512 devices in a mesh: plant: 8 (over x, y_hi), section: 64 (over y_lo, z, core).
Axes of the slice: x: 4, y: 8 (y_hi: 2, y_lo: 4; y = y_hi * 4 + y_lo), z: 8, core: 2. Of those that a mesh axis runs over, the one named last changes fastest.
Arguments:
- dynamics_operator: bfloat16 [4096, 512], P('plant'), parts along dimension 0
- control_gain_array: bfloat16 [4096, 256], P('plant'), parts along dimension 0
- kkt_inverse: bfloat16 [6144, 768], P('plant'), parts along dimension 0
- lin_state: float32 [4096, 16384], P(('plant', 'section')), parts along dimension 0, may hold values from -6 to 6
- lin_input: float32 [2048, 16384], P(('plant', 'section')), parts along dimension 0, may hold values from -6 to 6
- block_start: int32 [8], P('plant'), parts along dimension 0, may hold values from 0 to 63
- period: int32 [8], P('plant'), parts along dimension 0, may hold values from 8192 to 16384
Outputs:
- state_traj: float32 [4096, 16384], P('plant', 'section'), parts along dimension 0
- input_traj: float32 [2048, 16384], P('plant', 'section'), parts along dimension 0
- consensus: float32 [4096, 16384], P('plant', 'section'), parts along dimension 0
- residual_norms: float32 [16], P('plant'), parts along dimension 0
The draws below stay inside these ranges and needn't reach their ends.
There are 8 independent parts, one for each index of `plant`. The reference program is written for one: setup_inputs(seed, part) draws one part's arguments, and reference() takes and returns one part's arrays. A program takes and returns all parts, laid end to end along the dimension named above; each array names one. Nothing has to cross between parts.
Inputs may be any that keep to these rules, and one draw needn't show every extreme that they name: Device d of the section axis holds the block of logical sections starting at 256 * ((d - block_start) mod the axis's size).
All inputs are finite; a program needn't handle non-finite values.
Results may differ from the reference program's by a relative error of at most 0.0045.
Values sent between devices are 32-bit elements; how exact they have to be, the bound alone decides.
No kernel may reach another device: no remote copies, remote signals or barrier semaphores. Data moves between devices by JAX's collectives and lax.ppermute only.
A program may use at most 64 MiB of HBM per device.

```python
import jax
import jax.numpy as jnp
from jax import lax

STATE = 512
INPUT = 256
ITERS = 4
SECTIONS = 16384
N_SECTION = 64


RHO = 1.0


def plant_system(key):
    key_a = jax.random.fold_in(key, 11)
    key_b = jax.random.fold_in(key, 23)
    key_state = jax.random.fold_in(key, 37)
    key_input = jax.random.fold_in(key, 41)
    dynamics_operator = (jax.random.normal(key_a, (STATE, STATE), jnp.float32) / jnp.sqrt(jnp.float32(STATE))).astype(jnp.bfloat16)
    control_gain_array = (jax.random.normal(key_b, (STATE, INPUT), jnp.float32) / jnp.sqrt(jnp.float32(INPUT))).astype(jnp.bfloat16)
    low_end, high_end = (0.5, 5.0)
    state_weight = jnp.exp(jax.random.uniform(key_state, (STATE,), jnp.float32, jnp.log(low_end), jnp.log(high_end)))
    input_weight = jnp.exp(jax.random.uniform(key_input, (INPUT,), jnp.float32, jnp.log(0.1), jnp.log(1.0)))
    merged_pieces = jnp.concatenate([dynamics_operator, control_gain_array], axis=1).astype(jnp.float32)
    hessian = RHO * jnp.dot(merged_pieces.T, merged_pieces, precision=lax.Precision.HIGHEST)
    hessian = hessian + jnp.diag(jnp.concatenate([state_weight + RHO, input_weight]))
    inverse = jnp.linalg.inv(hessian)
    return (dynamics_operator, control_gain_array, inverse.astype(jnp.bfloat16))


def draw_dynamics_operator(key, part):
    return plant_system(key)[0]


def draw_control_gain_array(key, part):
    return plant_system(key)[1]


def draw_kkt_inverse(key, part):
    return plant_system(key)[2]


def levels(stream_key, shape, cuts, smallest, largest):
    def one(position, shards_of):
        steps = jax.random.uniform(jax.random.fold_in(jax.random.fold_in(stream_key, 6), position), (shards_of,), jnp.float32, smallest / len(cuts), largest / len(cuts))
        return jnp.repeat(jnp.exp(steps), shape[position] // shards_of).reshape((-1,) + (1,) * (len(shape) - position - 1))

    loudness = one(*cuts[0])
    for cut in cuts[1:]:
        loudness = loudness * one(*cut)
    return loudness


def noise(rng, shape, scale, most, split=(), kind=jnp.bfloat16):
    factor_of = levels(rng, shape, split, -0.22, 0.18) if split else 1.0
    entries = jax.random.normal(rng, shape, jnp.float32) * scale * factor_of
    return jnp.minimum(jnp.maximum(entries, -most), most).astype(kind)


def setup_inputs(seed: int = 0, part: int = 0) -> dict:
    key_of = jax.random.split(jax.random.key(seed), 8)
    own_keys = jax.random.split(jax.random.fold_in(key_of[7], part), 8)
    return {
        "dynamics_operator": draw_dynamics_operator(jax.random.fold_in(jax.random.fold_in(key_of[7], part), 71), part),
        "control_gain_array": draw_control_gain_array(jax.random.fold_in(jax.random.fold_in(key_of[7], part), 71), part),
        "kkt_inverse": draw_kkt_inverse(jax.random.fold_in(jax.random.fold_in(key_of[7], part), 71), part),
        "lin_state": noise(own_keys[3], (STATE, SECTIONS), 1.0, 6.0, ((0, 64),), jnp.float32),
        "lin_input": noise(own_keys[4], (INPUT, SECTIONS), 1.0, 6.0, ((0, 64),), jnp.float32),
        "block_start": jax.random.randint(own_keys[5], (1,), 0, N_SECTION).astype(jnp.int32),
        "period": jax.random.randint(own_keys[6], (1,), SECTIONS // 2, SECTIONS + 1).astype(jnp.int32),
    }


RHO = 1.0

def adjoint(dynamics_operator, control_gain_array, target):
    rounded = target.astype(jnp.bfloat16)
    contract = (((0,), (0,)), ((), ()))
    upper_part = lax.dot_general(dynamics_operator.astype(jnp.float32), rounded.astype(jnp.float32), contract, preferred_element_type=jnp.float32)
    lower_part = lax.dot_general(control_gain_array.astype(jnp.float32), rounded.astype(jnp.float32), contract, preferred_element_type=jnp.float32)
    return jnp.concatenate([upper_part, lower_part], axis=0)

def estimate_condition(dynamics_operator, control_gain_array, merged_pieces, condition_lines):
    rounded = merged_pieces.astype(jnp.bfloat16)
    return jnp.dot(dynamics_operator.astype(jnp.float32), rounded[:condition_lines].astype(jnp.float32), preferred_element_type=jnp.float32) + jnp.dot(control_gain_array.astype(jnp.float32), rounded[condition_lines:].astype(jnp.float32), preferred_element_type=jnp.float32)

def reference(dynamics_operator, control_gain_array, kkt_inverse, lin_state, lin_input, block_start, period):
    condition_lines = dynamics_operator.shape[0]
    block_width = lin_state.shape[1] // N_SECTION
    offset = (block_start[0] * block_width).astype(jnp.int32)
    neg_cost = -jnp.concatenate([jnp.roll(lin_state, -offset, 1), jnp.roll(lin_input, -offset, 1)], axis=0)
    section_total = neg_cost.shape[1]
    section_ids = jnp.arange(section_total, dtype=jnp.int32)
    working_segment = (section_ids < period[0])[None, :]
    is_first = (section_ids == 0)[None, :]
    stop_index = (period[0] - 1).astype(jnp.int32)
    is_last = (section_ids == stop_index)[None, :]
    zero_block = jnp.zeros((condition_lines, section_total), jnp.float32)
    input_zero = jnp.zeros((neg_cost.shape[0] - condition_lines, section_total), jnp.float32)
    consensus = zero_block
    dual_state = zero_block
    multiplier_link = zero_block
    ahead_z = zero_block
    feasibility_gap_total = jnp.float32(0.0)
    dual_sum = jnp.float32(0.0)
    merged_pieces = jnp.zeros_like(neg_cost)
    for iteration in range(ITERS):
        right_side = neg_cost + RHO * jnp.concatenate([consensus - dual_state, input_zero], axis=0) + RHO * adjoint(dynamics_operator, control_gain_array, ahead_z - multiplier_link)
        product = jnp.dot(kkt_inverse.astype(jnp.float32), right_side.astype(jnp.bfloat16).astype(jnp.float32), preferred_element_type=jnp.float32)
        merged_pieces = jnp.where(working_segment, product, 0.0)
        expected_condition = estimate_condition(dynamics_operator, control_gain_array, merged_pieces, condition_lines)
        own_sum = merged_pieces[:condition_lines] + dual_state
        passed_quantity = expected_condition + multiplier_link
        previous = jnp.roll(passed_quantity, 1, axis=1)
        closing_carried = lax.dynamic_slice_in_dim(passed_quantity, stop_index, 1, 1)
        previous = jnp.where(is_first, closing_carried, previous)
        newest_agreement = jnp.where(working_segment, 0.5 * (own_sum + previous), 0.0)
        onward_refreshed = jnp.where(is_last, newest_agreement[:, 0:1], jnp.roll(newest_agreement, -1, axis=1))
        change_z = newest_agreement - consensus
        dual_state = jnp.where(working_segment, dual_state + merged_pieces[:condition_lines] - newest_agreement, 0.0)
        multiplier_link = jnp.where(working_segment, multiplier_link + expected_condition - onward_refreshed, 0.0)
        feasibility_gap_total = jnp.sum(jnp.where(working_segment, (merged_pieces[:condition_lines] - newest_agreement) ** 2 + (expected_condition - onward_refreshed) ** 2, 0.0))
        dual_sum = RHO * RHO * jnp.sum(change_z * change_z)
        consensus = newest_agreement
        ahead_z = onward_refreshed
    state_traj = jnp.roll(merged_pieces[:condition_lines], offset, 1)
    input_traj = jnp.roll(merged_pieces[condition_lines:], offset, 1)
    consensus_out = jnp.roll(consensus, offset, 1)
    residual_norms = jnp.stack([jnp.sqrt(feasibility_gap_total), jnp.sqrt(dual_sum)]).astype(jnp.float32)
    return (state_traj, input_traj, consensus_out, residual_norms)
```

```python
import jax
import jax.numpy as jnp
from jax import lax
from jax.experimental import pallas as pl
from jax.experimental.pallas import tpu as pltpu
from jax.sharding import PartitionSpec as P

ITERS = 4
RHO = 1.0
LANES = 128
HALO = 4


def pack(block_start, period, state, inputs, parts):
    rows_state, total = state.shape
    rows_input = inputs.shape[0]
    width = total // parts
    per = 2 * rows_state + 2 * rows_input + 1
    assert width == 2 * LANES and rows_state == 8 and rows_input == 4

    def body(bs_ref, pe_ref, st_ref, in_ref, out_ref, flat_ref, halo_ref):
        bs = bs_ref[0]
        pe = pe_ref[0]
        lane = lax.broadcasted_iota(jnp.int32, (16, LANES), 1)

        def tile(position):
            at = pl.ds(pl.multiple_of(position, LANES), LANES)
            return jnp.concatenate(
                [st_ref[:, at], in_ref[:, at], jnp.zeros((4, LANES), jnp.float32)], axis=0
            )

        first = tile(bs * width)
        onward = pltpu.roll(first, lax.rem(pe, LANES), 1)
        edges = []
        for q in range(4):
            collected = jnp.zeros((16, LANES), jnp.float32)
            for e in range(16):
                d = 16 * q + e
                ends = []
                for half in range(2):
                    at = (2 * d + half) * LANES
                    section = lax.rem(at - bs * width + total, total)
                    beyond = lane + (section - pe)
                    wraps = (beyond >= 0) & (beyond < HALO)
                    cut = jnp.where(wraps, onward, tile(at))
                    out_ref[per * d + 8 * half : per * d + 8 * half + 8, :] = cut[:8]
                    out_ref[per * d + 16 + 4 * half : per * d + 20 + 4 * half, :] = cut[8:12]
                    ends.append(cut)
                both = jnp.where(lane < HALO, ends[0], ends[1])
                shift = (8 * e + HALO) % LANES
                both = pltpu.roll(both, shift, 1) if shift else both
                collected = jnp.where((lane >> 3) == e, both, collected)
            edges.append(collected)
        before = lax.rem(bs + parts - 1, parts)
        late = lax.rem(pe - HALO, LANES)
        tail_at = lax.rem(pe - HALO - late + bs * width, total)
        tail_next = lax.rem(tail_at + LANES, total)
        tail = jnp.where(lane >= late, tile(tail_at), tile(tail_next))
        tail = pltpu.roll(tail, lax.rem(8 * lax.rem(before, 16) - late + LANES, LANES), 1)
        skip = total - pe
        skip = jnp.where(skip < HALO, skip, 0)
        head = pltpu.roll(first, lax.rem(8 * lax.rem(bs, 16) + HALO - skip + LANES, LANES), 1)
        for q in range(4):
            block = 16 * q + (lane >> 3)
            slot = lane & 7
            value = jnp.where((block == before) & (slot < HALO), tail, edges[q])
            value = jnp.where((block == bs) & (slot >= HALO), head, value)
            flat_ref[LANES * q : LANES * q + LANES, 0:16] = value.T
        for h in range(8):
            halo_ref[:, 16 * h : 16 * h + 16] = flat_ref[pl.ds(h, parts, stride=8), 0:16]
        flat = halo_ref[...]
        lane = lax.broadcasted_iota(jnp.int32, (parts, LANES), 1)
        out_ref[pl.ds(per - 1, parts, stride=per), :] = jnp.where(
            lane < 64, pltpu.roll(flat, 1, 0), pltpu.roll(flat, parts - 1, 0)
        )

    smem = pl.BlockSpec(memory_space=pltpu.SMEM)
    vmem = pl.BlockSpec(memory_space=pltpu.VMEM)
    return pl.pallas_call(
        body,
        name="pack",
        out_shape=jax.ShapeDtypeStruct((parts * per, LANES), jnp.float32),
        in_specs=[smem, smem, vmem, vmem],
        out_specs=vmem,
        scratch_shapes=[
            pltpu.VMEM((4 * LANES, LANES), jnp.float32),
            pltpu.VMEM((parts, LANES), jnp.float32),
        ],
        compiler_params=pltpu.CompilerParams(vmem_limit_bytes=32 << 20),
    )(block_start, period, state, inputs)


def iterate(block_start, period, received, dynamics, gain, inverse, parts):
    states = dynamics.shape[0]
    controls = gain.shape[1]
    both = states + controls
    width = 2 * LANES
    rows = width + 2 * HALO
    per = received.shape[0] // parts
    nt = (((1,), (1,)), ((), ()))
    nn = (((1,), (0,)), ((), ()))
    tn = (((0,), (0,)), ((), ()))

    def body(bs_ref, pe_ref, got_ref, a_ref, b_ref, k_ref, x_ref, u_ref, z_ref, sums_ref,
             neg_ref, w_ref, zs_ref, ys_ref, vs_ref, gn_ref):
        sub = lax.broadcasted_iota(jnp.int32, (8, LANES), 0)
        for g in range(states // LANES):
            for j in range(2):
                block = jnp.concatenate(
                    [got_ref[per * s + 8 * j : per * s + 8 * j + 8, :] for s in range(16 * g, 16 * g + 16)], axis=0
                )
                neg_ref[LANES * j : LANES * j + LANES, LANES * g : LANES * g + LANES] = -block.T
        for g in range(controls // LANES):
            halves = ([], [])
            for s in range(32 * g, 32 * g + 32, 2):
                one = got_ref[per * s + 16 : per * s + 24, :]
                two = got_ref[per * (s + 1) + 16 : per * (s + 1) + 24, :]
                halves[0].append(jnp.where(sub < 4, one, pltpu.roll(two, 4, 0)))
                halves[1].append(jnp.where(sub < 4, pltpu.roll(one, 4, 0), two))
            for j in range(2):
                at = states + LANES * g
                neg_ref[LANES * j : LANES * j + LANES, at : at + LANES] = -jnp.concatenate(halves[j], axis=0).T
        edge = got_ref[pl.ds(per - 1, parts, stride=per), :]
        high = edge.astype(jnp.bfloat16)
        rest = edge - high.astype(jnp.float32)
        middle = rest.astype(jnp.bfloat16)
        low = (rest - middle.astype(jnp.float32)).astype(jnp.bfloat16)
        cut = jnp.concatenate([high, middle, low], axis=0)
        src = lax.broadcasted_iota(jnp.int32, (3 * parts, both), 0) & (parts - 1)
        col = lax.broadcasted_iota(jnp.int32, (3 * parts, both), 1)
        owner = jnp.where(col < states, col >> 3, (col - states) >> 2)
        spread = jnp.where(owner == src, 1.0, 0.0).astype(jnp.bfloat16)
        wide = lax.dot_general(cut, spread, tn, preferred_element_type=jnp.float32)
        slot = lax.broadcasted_iota(jnp.int32, (LANES, both), 0) & 15
        col = lax.broadcasted_iota(jnp.int32, (LANES, both), 1)
        place = jnp.where(col < states, col & 7, 8 + (col & 3))
        wide = jnp.where(slot == place, wide, 0.0).reshape(8, 16, both).sum(axis=1)
        neg_ref[width : width + 8, :] = -pltpu.roll(wide, HALO, 0)

        for it in range(ITERS):
            last = it == ITERS - 1
            if it == 0:
                rhs = neg_ref[...].astype(jnp.bfloat16)
            else:
                g = gn_ref[...]
                t_s = lax.dot_general(g, a_ref[...], nn, preferred_element_type=jnp.float32)
                t_u = lax.dot_general(g, b_ref[...], nn, preferred_element_type=jnp.float32)
                rhs = jnp.concatenate(
                    [
                        (neg_ref[:, :states] + RHO * (zs_ref[...] - ys_ref[...]) + RHO * t_s).astype(jnp.bfloat16),
                        (neg_ref[:, states:] + RHO * t_u).astype(jnp.bfloat16),
                    ],
                    axis=1,
                )
            w = lax.dot_general(rhs, k_ref[...], nt, preferred_element_type=jnp.float32)
            x = w[:, :states]
            wb = w.astype(jnp.bfloat16)
            pred = lax.dot_general(wb[:, :states], a_ref[...], nt, preferred_element_type=jnp.float32)
            pred = pred + lax.dot_general(wb[:, states:], b_ref[...], nt, preferred_element_type=jnp.float32)
            if it == 0:
                a, p = x, pred
            else:
                a, p = x + ys_ref[...], pred + vs_ref[...]
            znew = 0.5 * (a + pltpu.roll(p, 1, 0))
            znn = pltpu.roll(znew, rows - 1, 0)
            if not last:
                ys_ref[...] = a - znew
                v = p - znn
                vs_ref[...] = v
                gn_ref[...] = (znn - v).astype(jnp.bfloat16)
                zs_ref[...] = znew
            else:
                idx = lax.rem(lax.axis_index("section") - bs_ref[0] + parts, parts)
                count = pe_ref[0] - idx * width
                here = lax.broadcasted_iota(jnp.int32, (width, states), 0) < count
                gap = (x - znew)[:width]
                miss = (pred - znn)[:width]
                step = znew[:width] - zs_ref[:width, :]
                primal = jnp.sum(jnp.where(here, gap * gap + miss * miss, 0.0))
                dual = RHO * RHO * jnp.sum(jnp.where(here, step * step, 0.0))
                lane = lax.broadcasted_iota(jnp.int32, (parts, LANES), 1)
                sums_ref[...] = jnp.where(lane == 0, primal, jnp.where(lane == 1, dual, 0.0))
                keep = lax.broadcasted_iota(jnp.int32, (states, width), 1) < count
                x_ref[...] = jnp.where(keep, x[:width].T, 0.0)
                z_ref[...] = jnp.where(keep, znew[:width].T, 0.0)
                u_ref[...] = jnp.where(keep[:controls], w[:width, states:].T, 0.0)

    smem = pl.BlockSpec(memory_space=pltpu.SMEM)
    vmem = pl.BlockSpec(memory_space=pltpu.VMEM)
    return pl.pallas_call(
        body,
        name="iterate",
        out_shape=(
            jax.ShapeDtypeStruct((states, width), jnp.float32),
            jax.ShapeDtypeStruct((controls, width), jnp.float32),
            jax.ShapeDtypeStruct((states, width), jnp.float32),
            jax.ShapeDtypeStruct((parts, LANES), jnp.float32),
        ),
        in_specs=[smem, smem, vmem, vmem, vmem, vmem],
        out_specs=(vmem, vmem, vmem, vmem),
        scratch_shapes=[
            pltpu.VMEM((rows, both), jnp.float32),
            pltpu.VMEM((rows, both), jnp.float32),
            pltpu.VMEM((rows, states), jnp.float32),
            pltpu.VMEM((rows, states), jnp.float32),
            pltpu.VMEM((rows, states), jnp.float32),
            pltpu.VMEM((rows, states), jnp.bfloat16),
        ],
        compiler_params=pltpu.CompilerParams(vmem_limit_bytes=48 << 20),
    )(block_start, period, received, dynamics, gain, inverse)


def swap(rows, parts):
    flat = rows.reshape(parts, 1, rows.size // parts)
    return lax.all_to_all(flat, "section", 0, 0, tiled=True)


def local(dynamics, gain, inverse, lin_state, lin_input, block_start, period):
    parts = lax.axis_size("section")
    packed = pack(block_start, period, lin_state, lin_input, parts)
    received = swap(packed, parts).reshape(packed.shape)
    x, u, z, sums = iterate(block_start, period, received, dynamics, gain, inverse, parts)
    sums = swap(sums, parts)
    return x, u, z, jnp.sqrt(jnp.sum(sums[:, 0, :2], axis=0))


def solution(mesh):
    return jax.shard_map(
        local,
        mesh=mesh,
        in_specs=(
            P("plant", None),
            P("plant", None),
            P("plant", None),
            P(("plant", "section"), None),
            P(("plant", "section"), None),
            P("plant"),
            P("plant"),
        ),
        out_specs=(P("plant", "section"), P("plant", "section"), P("plant", "section"), P("plant")),
        check_vma=False,
    )
```

```python
import jax
import jax.numpy as jnp
from jax import lax
from jax.experimental import pallas as pl
from jax.experimental.pallas import tpu as pltpu
from jax.sharding import PartitionSpec as P

ITERS = 4
RHO = 1.0
LANES = 128
HALO = 4


def pack(block_start, period, state, inputs, parts):
    rows_state, total = state.shape
    rows_input = inputs.shape[0]
    width = total // parts
    per = 2 * rows_state + 2 * rows_input + 1
    assert width == 2 * LANES and rows_state == 8 and rows_input == 4

    pieces = 2
    piece = total // pieces

    def body(bs_ref, pe_ref, st_hbm, in_hbm, out_ref, st_ref, in_ref, st_first, in_first, flat_ref, halo_ref, sems):
        bs = bs_ref[0]
        pe = pe_ref[0]
        opening = pl.ds(pl.multiple_of(bs * width, LANES), LANES)
        copies = [
            pltpu.make_async_copy(st_hbm.at[:, opening], st_first, sems.at[0]),
            pltpu.make_async_copy(in_hbm.at[:, opening], in_first, sems.at[1]),
        ]
        for q in range(pieces):
            at = slice(piece * q, piece * q + piece)
            copies.append(pltpu.make_async_copy(st_hbm.at[:, at], st_ref.at[:, at], sems.at[2 + 2 * q]))
            copies.append(pltpu.make_async_copy(in_hbm.at[:, at], in_ref.at[:, at], sems.at[3 + 2 * q]))
        for copy in copies:
            copy.start()
        lane = lax.broadcasted_iota(jnp.int32, (16, LANES), 1)
        spare = jnp.zeros((4, LANES), jnp.float32)

        def tile(position):
            at = pl.ds(pl.multiple_of(position, LANES), LANES)
            return jnp.concatenate([st_ref[:, at], in_ref[:, at], spare], axis=0)

        copies[0].wait()
        copies[1].wait()
        first = jnp.concatenate([st_first[...], in_first[...], spare], axis=0)
        onward = pltpu.roll(first, lax.rem(pe, LANES), 1)
        edges = []
        for q in range(4):
            if q * pieces % 4 == 0:
                copies[2 + 2 * (q * pieces // 4)].wait()
                copies[3 + 2 * (q * pieces // 4)].wait()
            collected = jnp.zeros((16, LANES), jnp.float32)
            for e in range(16):
                d = 16 * q + e
                ends = []
                for half in range(2):
                    at = (2 * d + half) * LANES
                    section = lax.rem(at - bs * width + total, total)
                    beyond = lane + (section - pe)
                    wraps = (beyond >= 0) & (beyond < HALO)
                    cut = jnp.where(wraps, onward, tile(at))
                    out_ref[per * d + 8 * half : per * d + 8 * half + 8, :] = cut[:8]
                    out_ref[per * d + 16 + 4 * half : per * d + 20 + 4 * half, :] = cut[8:12]
                    ends.append(cut)
                both = jnp.where(lane < HALO, ends[0], ends[1])
                shift = (8 * e + HALO) % LANES
                both = pltpu.roll(both, shift, 1) if shift else both
                collected = jnp.where((lane >> 3) == e, both, collected)
            edges.append(collected)
        before = lax.rem(bs + parts - 1, parts)
        late = lax.rem(pe - HALO, LANES)
        tail_at = lax.rem(pe - HALO - late + bs * width, total)
        tail_next = lax.rem(tail_at + LANES, total)
        tail = jnp.where(lane >= late, tile(tail_at), tile(tail_next))
        tail = pltpu.roll(tail, lax.rem(8 * lax.rem(before, 16) - late + LANES, LANES), 1)
        skip = total - pe
        skip = jnp.where(skip < HALO, skip, 0)
        head = pltpu.roll(first, lax.rem(8 * lax.rem(bs, 16) + HALO - skip + LANES, LANES), 1)
        for q in range(4):
            block = 16 * q + (lane >> 3)
            slot = lane & 7
            value = jnp.where((block == before) & (slot < HALO), tail, edges[q])
            value = jnp.where((block == bs) & (slot >= HALO), head, value)
            flat_ref[LANES * q : LANES * q + LANES, 0:16] = value.T
        for h in range(8):
            halo_ref[:, 16 * h : 16 * h + 16] = flat_ref[pl.ds(h, parts, stride=8), 0:16]
        flat = halo_ref[...]
        lane = lax.broadcasted_iota(jnp.int32, (parts, LANES), 1)
        out_ref[pl.ds(per - 1, parts, stride=per), :] = jnp.where(
            lane < 64, pltpu.roll(flat, 1, 0), pltpu.roll(flat, parts - 1, 0)
        )

    smem = pl.BlockSpec(memory_space=pltpu.SMEM)
    vmem = pl.BlockSpec(memory_space=pltpu.VMEM)
    hbm = pl.BlockSpec(memory_space=pltpu.HBM)
    return pl.pallas_call(
        body,
        name="pack",
        out_shape=jax.ShapeDtypeStruct((parts * per, LANES), jnp.float32),
        in_specs=[smem, smem, hbm, hbm],
        out_specs=vmem,
        scratch_shapes=[
            pltpu.VMEM(state.shape, jnp.float32),
            pltpu.VMEM(inputs.shape, jnp.float32),
            pltpu.VMEM((rows_state, LANES), jnp.float32),
            pltpu.VMEM((rows_input, LANES), jnp.float32),
            pltpu.VMEM((4 * LANES, LANES), jnp.float32),
            pltpu.VMEM((parts, LANES), jnp.float32),
            pltpu.SemaphoreType.DMA((2 + 2 * pieces,)),
        ],
        compiler_params=pltpu.CompilerParams(vmem_limit_bytes=32 << 20),
    )(
        block_start,
        period,
        pltpu.with_memory_space_constraint(state, pltpu.HBM),
        pltpu.with_memory_space_constraint(inputs, pltpu.HBM),
    )


def iterate(block_start, period, received, dynamics, gain, inverse, parts):
    states = dynamics.shape[0]
    controls = gain.shape[1]
    both = states + controls
    width = 2 * LANES
    rows = width + 2 * HALO
    per = received.shape[0] // parts
    nt = (((1,), (1,)), ((), ()))
    nn = (((1,), (0,)), ((), ()))
    tn = (((0,), (0,)), ((), ()))

    def body(bs_ref, pe_ref, got_ref, a_ref, b_ref, k_ref, x_ref, u_ref, z_ref, sums_ref,
             neg_ref, w_ref, zs_ref, ys_ref, vs_ref, gn_ref):
        sub = lax.broadcasted_iota(jnp.int32, (8, LANES), 0)
        for g in range(states // LANES):
            for j in range(2):
                block = jnp.concatenate(
                    [got_ref[per * s + 8 * j : per * s + 8 * j + 8, :] for s in range(16 * g, 16 * g + 16)], axis=0
                )
                neg_ref[LANES * j : LANES * j + LANES, LANES * g : LANES * g + LANES] = -block.T
        for g in range(controls // LANES):
            halves = ([], [])
            for s in range(32 * g, 32 * g + 32, 2):
                one = got_ref[per * s + 16 : per * s + 24, :]
                two = got_ref[per * (s + 1) + 16 : per * (s + 1) + 24, :]
                halves[0].append(jnp.where(sub < 4, one, pltpu.roll(two, 4, 0)))
                halves[1].append(jnp.where(sub < 4, pltpu.roll(one, 4, 0), two))
            for j in range(2):
                at = states + LANES * g
                neg_ref[LANES * j : LANES * j + LANES, at : at + LANES] = -jnp.concatenate(halves[j], axis=0).T
        edge = got_ref[pl.ds(per - 1, parts, stride=per), :]
        high = edge.astype(jnp.bfloat16)
        rest = edge - high.astype(jnp.float32)
        middle = rest.astype(jnp.bfloat16)
        low = (rest - middle.astype(jnp.float32)).astype(jnp.bfloat16)
        cut = jnp.concatenate([high, middle, low], axis=0)
        src = lax.broadcasted_iota(jnp.int32, (3 * parts, both), 0) & (parts - 1)
        col = lax.broadcasted_iota(jnp.int32, (3 * parts, both), 1)
        owner = jnp.where(col < states, col >> 3, (col - states) >> 2)
        spread = jnp.where(owner == src, 1.0, 0.0).astype(jnp.bfloat16)
        wide = lax.dot_general(cut, spread, tn, preferred_element_type=jnp.float32)
        slot = lax.broadcasted_iota(jnp.int32, (LANES, both), 0) & 15
        col = lax.broadcasted_iota(jnp.int32, (LANES, both), 1)
        place = jnp.where(col < states, col & 7, 8 + (col & 3))
        wide = jnp.where(slot == place, wide, 0.0).reshape(8, 16, both).sum(axis=1)
        neg_ref[width : width + 8, :] = -pltpu.roll(wide, HALO, 0)

        for it in range(ITERS):
            last = it == ITERS - 1
            if it == 0:
                rhs = neg_ref[...].astype(jnp.bfloat16)
            else:
                g = gn_ref[...]
                t_s = lax.dot_general(g, a_ref[...], nn, preferred_element_type=jnp.float32)
                t_u = lax.dot_general(g, b_ref[...], nn, preferred_element_type=jnp.float32)
                rhs = jnp.concatenate(
                    [
                        (neg_ref[:, :states] + RHO * (zs_ref[...] - ys_ref[...]) + RHO * t_s).astype(jnp.bfloat16),
                        (neg_ref[:, states:] + RHO * t_u).astype(jnp.bfloat16),
                    ],
                    axis=1,
                )
            w = lax.dot_general(rhs, k_ref[...], nt, preferred_element_type=jnp.float32)
            x = w[:, :states]
            wb = w.astype(jnp.bfloat16)
            pred = lax.dot_general(wb[:, :states], a_ref[...], nt, preferred_element_type=jnp.float32)
            pred = pred + lax.dot_general(wb[:, states:], b_ref[...], nt, preferred_element_type=jnp.float32)
            if it == 0:
                a, p = x, pred
            else:
                a, p = x + ys_ref[...], pred + vs_ref[...]
            znew = 0.5 * (a + pltpu.roll(p, 1, 0))
            znn = pltpu.roll(znew, rows - 1, 0)
            if not last:
                ys_ref[...] = a - znew
                v = p - znn
                vs_ref[...] = v
                gn_ref[...] = (znn - v).astype(jnp.bfloat16)
                zs_ref[...] = znew
            else:
                idx = lax.rem(lax.axis_index("section") - bs_ref[0] + parts, parts)
                count = pe_ref[0] - idx * width
                here = lax.broadcasted_iota(jnp.int32, (width, states), 0) < count
                gap = (x - znew)[:width]
                miss = (pred - znn)[:width]
                step = znew[:width] - zs_ref[:width, :]
                primal = jnp.sum(jnp.where(here, gap * gap + miss * miss, 0.0))
                dual = RHO * RHO * jnp.sum(jnp.where(here, step * step, 0.0))
                lane = lax.broadcasted_iota(jnp.int32, (parts, LANES), 1)
                sums_ref[...] = jnp.where(lane == 0, primal, jnp.where(lane == 1, dual, 0.0))
                keep = lax.broadcasted_iota(jnp.int32, (states, width), 1) < count
                x_ref[...] = jnp.where(keep, x[:width].T, 0.0)
                z_ref[...] = jnp.where(keep, znew[:width].T, 0.0)
                u_ref[...] = jnp.where(keep[:controls], w[:width, states:].T, 0.0)

    smem = pl.BlockSpec(memory_space=pltpu.SMEM)
    vmem = pl.BlockSpec(memory_space=pltpu.VMEM)
    return pl.pallas_call(
        body,
        name="iterate",
        out_shape=(
            pltpu.VMEM((states, width), jnp.float32),
            pltpu.VMEM((controls, width), jnp.float32),
            pltpu.VMEM((states, width), jnp.float32),
            pltpu.VMEM((parts, LANES), jnp.float32),
        ),
        in_specs=[smem, smem, vmem, vmem, vmem, vmem],
        out_specs=(vmem, vmem, vmem, vmem),
        scratch_shapes=[
            pltpu.VMEM((rows, both), jnp.float32),
            pltpu.VMEM((rows, both), jnp.float32),
            pltpu.VMEM((rows, states), jnp.float32),
            pltpu.VMEM((rows, states), jnp.float32),
            pltpu.VMEM((rows, states), jnp.float32),
            pltpu.VMEM((rows, states), jnp.bfloat16),
        ],
        compiler_params=pltpu.CompilerParams(vmem_limit_bytes=48 << 20),
    )(block_start, period, received, dynamics, gain, inverse)


def swap(rows, parts):
    flat = rows.reshape(parts, 1, rows.size // parts)
    return lax.all_to_all(flat, "section", 0, 0, tiled=True)


def local(dynamics, gain, inverse, lin_state, lin_input, block_start, period):
    parts = lax.axis_size("section")
    packed = pack(block_start, period, lin_state, lin_input, parts)
    received = swap(packed, parts).reshape(packed.shape)
    x, u, z, sums = iterate(block_start, period, received, dynamics, gain, inverse, parts)
    sums = swap(sums, parts)
    return x, u, z, jnp.sqrt(jnp.sum(sums[:, 0, :2], axis=0))


def solution(mesh):
    return jax.shard_map(
        local,
        mesh=mesh,
        in_specs=(
            P("plant", None),
            P("plant", None),
            P("plant", None),
            P(("plant", "section"), None),
            P(("plant", "section"), None),
            P("plant"),
            P("plant"),
        ),
        out_specs=(P("plant", "section"), P("plant", "section"), P("plant", "section"), P("plant")),
        check_vma=False,
    )
```

```python
import jax
import jax.numpy as jnp
from jax import lax
from jax.experimental import pallas as pl
from jax.experimental.pallas import tpu as pltpu
from jax.sharding import PartitionSpec as P

ITERS = 4
RHO = 1.0
LANES = 128
HALO = 4


def pack(block_start, period, state, inputs, parts):
    rows_state, total = state.shape
    rows_input = inputs.shape[0]
    width = total // parts
    per = 2 * rows_state + 2 * rows_input + 1
    assert width == 2 * LANES and rows_state == 8 and rows_input == 4

    pieces = 2
    piece = total // pieces

    def body(bs_ref, pe_ref, st_hbm, in_hbm, out_ref, st_ref, in_ref, st_first, in_first, flat_ref, halo_ref, sems):
        bs = bs_ref[0]
        pe = pe_ref[0]
        opening = pl.ds(pl.multiple_of(bs * width, LANES), LANES)
        copies = [
            pltpu.make_async_copy(st_hbm.at[:, opening], st_first, sems.at[0]),
            pltpu.make_async_copy(in_hbm.at[:, opening], in_first, sems.at[1]),
        ]
        for q in range(pieces):
            at = slice(piece * q, piece * q + piece)
            copies.append(pltpu.make_async_copy(st_hbm.at[:, at], st_ref.at[:, at], sems.at[2 + 2 * q]))
            copies.append(pltpu.make_async_copy(in_hbm.at[:, at], in_ref.at[:, at], sems.at[3 + 2 * q]))
        for copy in copies:
            copy.start()
        lane = lax.broadcasted_iota(jnp.int32, (16, LANES), 1)
        spare = jnp.zeros((4, LANES), jnp.float32)

        def tile(position):
            at = pl.ds(pl.multiple_of(position, LANES), LANES)
            return jnp.concatenate([st_ref[:, at], in_ref[:, at], spare], axis=0)

        copies[0].wait()
        copies[1].wait()
        first = jnp.concatenate([st_first[...], in_first[...], spare], axis=0)
        onward = pltpu.roll(first, lax.rem(pe, LANES), 1)
        edges = []
        for q in range(4):
            if q * pieces % 4 == 0:
                copies[2 + 2 * (q * pieces // 4)].wait()
                copies[3 + 2 * (q * pieces // 4)].wait()
            collected = jnp.zeros((16, LANES), jnp.float32)
            for e in range(16):
                d = 16 * q + e
                ends = []
                for half in range(2):
                    at = (2 * d + half) * LANES
                    section = lax.rem(at - bs * width + total, total)
                    beyond = lane + (section - pe)
                    wraps = (beyond >= 0) & (beyond < HALO)
                    cut = jnp.where(wraps, onward, tile(at))
                    out_ref[per * d + 8 * half : per * d + 8 * half + 8, :] = cut[:8]
                    out_ref[per * d + 16 + 4 * half : per * d + 20 + 4 * half, :] = cut[8:12]
                    ends.append(cut)
                both = jnp.where(lane < HALO, ends[0], ends[1])
                shift = (8 * e + HALO) % LANES
                both = pltpu.roll(both, shift, 1) if shift else both
                collected = jnp.where((lane >> 3) == e, both, collected)
            edges.append(collected)
        before = lax.rem(bs + parts - 1, parts)
        late = lax.rem(pe - HALO, LANES)
        tail_at = lax.rem(pe - HALO - late + bs * width, total)
        tail_next = lax.rem(tail_at + LANES, total)
        tail = jnp.where(lane >= late, tile(tail_at), tile(tail_next))
        tail = pltpu.roll(tail, lax.rem(8 * lax.rem(before, 16) - late + LANES, LANES), 1)
        skip = total - pe
        skip = jnp.where(skip < HALO, skip, 0)
        head = pltpu.roll(first, lax.rem(8 * lax.rem(bs, 16) + HALO - skip + LANES, LANES), 1)
        for q in range(4):
            block = 16 * q + (lane >> 3)
            slot = lane & 7
            value = jnp.where((block == before) & (slot < HALO), tail, edges[q])
            value = jnp.where((block == bs) & (slot >= HALO), head, value)
            flat_ref[LANES * q : LANES * q + LANES, 0:16] = value.T
        for h in range(8):
            halo_ref[:, 16 * h : 16 * h + 16] = flat_ref[pl.ds(h, parts, stride=8), 0:16]
        flat = halo_ref[...]
        lane = lax.broadcasted_iota(jnp.int32, (parts, LANES), 1)
        out_ref[pl.ds(per - 1, parts, stride=per), :] = jnp.where(
            lane < 64, pltpu.roll(flat, 1, 0), pltpu.roll(flat, parts - 1, 0)
        )

    smem = pl.BlockSpec(memory_space=pltpu.SMEM)
    vmem = pl.BlockSpec(memory_space=pltpu.VMEM)
    hbm = pl.BlockSpec(memory_space=pltpu.HBM)
    return pl.pallas_call(
        body,
        name="pack",
        out_shape=jax.ShapeDtypeStruct((parts * per, LANES), jnp.float32),
        in_specs=[smem, smem, hbm, hbm],
        out_specs=vmem,
        scratch_shapes=[
            pltpu.VMEM(state.shape, jnp.float32),
            pltpu.VMEM(inputs.shape, jnp.float32),
            pltpu.VMEM((rows_state, LANES), jnp.float32),
            pltpu.VMEM((rows_input, LANES), jnp.float32),
            pltpu.VMEM((4 * LANES, LANES), jnp.float32),
            pltpu.VMEM((parts, LANES), jnp.float32),
            pltpu.SemaphoreType.DMA((2 + 2 * pieces,)),
        ],
        compiler_params=pltpu.CompilerParams(vmem_limit_bytes=32 << 20),
    )(
        block_start,
        period,
        pltpu.with_memory_space_constraint(state, pltpu.HBM),
        pltpu.with_memory_space_constraint(inputs, pltpu.HBM),
    )


def iterate(block_start, period, received, dynamics, gain, inverse, parts):
    states = dynamics.shape[0]
    controls = gain.shape[1]
    both = states + controls
    width = 2 * LANES
    rows = width + 2 * HALO
    span = states
    per = received.shape[0] // parts
    nt = (((1,), (1,)), ((), ()))
    nn = (((1,), (0,)), ((), ()))
    tn = (((0,), (0,)), ((), ()))

    def body(bs_ref, pe_ref, got_ref, a_ref, b_ref, k_ref, x_ref, u_ref, z_ref, sums_ref,
             neg_ref, nd_ref, zs_ref, ys_ref, vs_ref, gn_ref, ab_ref):
        sub = lax.broadcasted_iota(jnp.int32, (8, LANES), 0)
        for g in range(states // LANES):
            for j in range(2):
                block = jnp.concatenate(
                    [got_ref[per * s + 8 * j : per * s + 8 * j + 8, :] for s in range(16 * g, 16 * g + 16)], axis=0
                )
                neg_ref[LANES * j : LANES * j + LANES, LANES * g : LANES * g + LANES] = -block.T
        for g in range(controls // LANES):
            halves = ([], [])
            for s in range(32 * g, 32 * g + 32, 2):
                one = got_ref[per * s + 16 : per * s + 24, :]
                two = got_ref[per * (s + 1) + 16 : per * (s + 1) + 24, :]
                halves[0].append(jnp.where(sub < 4, one, pltpu.roll(two, 4, 0)))
                halves[1].append(jnp.where(sub < 4, pltpu.roll(one, 4, 0), two))
            for j in range(2):
                at = states + LANES * g
                neg_ref[LANES * j : LANES * j + LANES, at : at + LANES] = -jnp.concatenate(halves[j], axis=0).T
        edge = got_ref[pl.ds(per - 1, parts, stride=per), :]
        high = edge.astype(jnp.bfloat16)
        rest = edge - high.astype(jnp.float32)
        middle = rest.astype(jnp.bfloat16)
        low = (rest - middle.astype(jnp.float32)).astype(jnp.bfloat16)
        cut = jnp.concatenate([high, middle, low], axis=0)
        src = lax.broadcasted_iota(jnp.int32, (3 * parts, both), 0) & (parts - 1)
        col = lax.broadcasted_iota(jnp.int32, (3 * parts, both), 1)
        owner = jnp.where(col < states, col >> 3, (col - states) >> 2)
        spread = jnp.where(owner == src, 1.0, 0.0).astype(jnp.bfloat16)
        wide = lax.dot_general(cut, spread, tn, preferred_element_type=jnp.float32)
        slot = lax.broadcasted_iota(jnp.int32, (LANES, both), 0) & 15
        col = lax.broadcasted_iota(jnp.int32, (LANES, both), 1)
        place = jnp.where(col < states, col & 7, 8 + (col & 3))
        wide = jnp.where(slot == place, wide, 0.0).reshape(8, 16, both).sum(axis=1)
        neg_ref[width : width + 8, :] = -pltpu.roll(wide, HALO, 0)

        ab_ref[:, :states] = a_ref[...]
        ab_ref[:, states:] = b_ref[...]
        for it in range(ITERS):
            last = it == ITERS - 1
            if it == 0:
                rhs = neg_ref[...].astype(jnp.bfloat16)
            else:
                g = gn_ref[...]
                t = lax.dot_general(g, ab_ref[...], nn, preferred_element_type=jnp.float32)
                rhs = jnp.concatenate(
                    [
                        (nd_ref[...] + RHO * t[:, :states]).astype(jnp.bfloat16),
                        (neg_ref[:, states:] + RHO * t[:, states:]).astype(jnp.bfloat16),
                    ],
                    axis=1,
                )
            w = lax.dot_general(rhs, k_ref[...], nt, preferred_element_type=jnp.float32)
            wb = w.astype(jnp.bfloat16)
            primal, dual = 0.0, 0.0
            if last:
                idx = lax.rem(lax.axis_index("section") - bs_ref[0] + parts, parts)
                count = pe_ref[0] - idx * width
                here = lax.broadcasted_iota(jnp.int32, (width, span), 0) < count
                keep = lax.broadcasted_iota(jnp.int32, (states, width), 1) < count
                u_ref[...] = jnp.where(keep[:controls], w[:width, states:].T, 0.0)
            for n in range(0, states, span):
                at = slice(n, n + span)
                x = w[:, at]
                pred = lax.dot_general(wb, ab_ref[at, :], nt, preferred_element_type=jnp.float32)
                if it == 0:
                    a, p = x, pred
                else:
                    a, p = x + ys_ref[:, at], pred + vs_ref[:, at]
                znew = 0.5 * (a + pltpu.roll(p, 1, 0))
                znn = pltpu.roll(znew, rows - 1, 0)
                if not last:
                    y = a - znew
                    v = p - znn
                    ys_ref[:, at] = y
                    vs_ref[:, at] = v
                    gn_ref[:, at] = (znn - v).astype(jnp.bfloat16)
                    nd_ref[:, at] = neg_ref[:, at] + RHO * (znew - y)
                    if it == ITERS - 2:
                        zs_ref[:, at] = znew[:width]
                else:
                    gap = (x - znew)[:width]
                    miss = (pred - znn)[:width]
                    step = znew[:width] - zs_ref[:, at]
                    primal += jnp.sum(jnp.where(here, gap * gap + miss * miss, 0.0), axis=0, keepdims=True)
                    dual += RHO * RHO * jnp.sum(jnp.where(here, step * step, 0.0), axis=0, keepdims=True)
                    x_ref[at, :] = jnp.where(keep[at], x[:width].T, 0.0)
                    z_ref[at, :] = jnp.where(keep[at], znew[:width].T, 0.0)
            if last:
                lane = lax.broadcasted_iota(jnp.int32, (parts, LANES), 1)
                sums_ref[...] = jnp.where(lane == 0, jnp.sum(primal), jnp.where(lane == 1, jnp.sum(dual), 0.0))

    smem = pl.BlockSpec(memory_space=pltpu.SMEM)
    vmem = pl.BlockSpec(memory_space=pltpu.VMEM)
    return pl.pallas_call(
        body,
        name="iterate",
        out_shape=(
            pltpu.VMEM((states, width), jnp.float32),
            pltpu.VMEM((controls, width), jnp.float32),
            pltpu.VMEM((states, width), jnp.float32),
            pltpu.VMEM((parts, LANES), jnp.float32),
        ),
        in_specs=[smem, smem, vmem, vmem, vmem, vmem],
        out_specs=(vmem, vmem, vmem, vmem),
        scratch_shapes=[
            pltpu.VMEM((rows, both), jnp.float32),
            pltpu.VMEM((rows, states), jnp.float32),
            pltpu.VMEM((width, states), jnp.float32),
            pltpu.VMEM((rows, states), jnp.float32),
            pltpu.VMEM((rows, states), jnp.float32),
            pltpu.VMEM((rows, states), jnp.bfloat16),
            pltpu.VMEM((states, both), jnp.bfloat16),
        ],
        compiler_params=pltpu.CompilerParams(vmem_limit_bytes=48 << 20),
    )(block_start, period, received, dynamics, gain, inverse)


def swap(rows, parts):
    flat = rows.reshape(parts, 1, rows.size // parts)
    return lax.all_to_all(flat, "section", 0, 0, tiled=True)


def local(dynamics, gain, inverse, lin_state, lin_input, block_start, period):
    parts = lax.axis_size("section")
    packed = pack(block_start, period, lin_state, lin_input, parts)
    received = swap(packed, parts).reshape(packed.shape)
    x, u, z, sums = iterate(block_start, period, received, dynamics, gain, inverse, parts)
    sums = swap(sums, parts)
    return x, u, z, jnp.sqrt(jnp.sum(sums[:, 0, :2], axis=0))


def solution(mesh):
    return jax.shard_map(
        local,
        mesh=mesh,
        in_specs=(
            P("plant", None),
            P("plant", None),
            P("plant", None),
            P(("plant", "section"), None),
            P(("plant", "section"), None),
            P("plant"),
            P("plant"),
        ),
        out_specs=(P("plant", "section"), P("plant", "section"), P("plant", "section"), P("plant")),
        check_vma=False,
    )
```

```python
import jax
import jax.numpy as jnp
from jax import lax
from jax.experimental import pallas as pl
from jax.experimental.pallas import tpu as pltpu
from jax.sharding import PartitionSpec as P

ITERS = 4
RHO = 1.0
LANES = 128
HALO = 4


def pack(block_start, period, state, inputs, parts):
    rows_state, total = state.shape
    rows_input = inputs.shape[0]
    width = total // parts
    per = 2 * rows_state + 2 * rows_input + 1
    assert width == 2 * LANES and rows_state == 8 and rows_input == 4

    pieces = 2
    piece = total // pieces

    def body(bs_ref, pe_ref, st_hbm, in_hbm, out_ref, st_ref, in_ref, st_first, in_first, flat_ref, sems):
        bs = bs_ref[0]
        pe = pe_ref[0]
        opening = pl.ds(pl.multiple_of(bs * width, LANES), LANES)
        copies = [
            pltpu.make_async_copy(st_hbm.at[:, opening], st_first, sems.at[0]),
            pltpu.make_async_copy(in_hbm.at[:, opening], in_first, sems.at[1]),
        ]
        for q in range(pieces):
            at = slice(piece * q, piece * q + piece)
            copies.append(pltpu.make_async_copy(st_hbm.at[:, at], st_ref.at[:, at], sems.at[2 + 2 * q]))
            copies.append(pltpu.make_async_copy(in_hbm.at[:, at], in_ref.at[:, at], sems.at[3 + 2 * q]))
        for copy in copies:
            copy.start()
        lane = lax.broadcasted_iota(jnp.int32, (16, LANES), 1)
        spare = jnp.zeros((4, LANES), jnp.float32)

        def tile(position):
            at = pl.ds(pl.multiple_of(position, LANES), LANES)
            return jnp.concatenate([st_ref[:, at], in_ref[:, at], spare], axis=0)

        copies[0].wait()
        copies[1].wait()
        first = jnp.concatenate([st_first[...], in_first[...], spare], axis=0)
        onward = pltpu.roll(first, lax.rem(pe, LANES), 1)
        edges = []
        for q in range(4):
            if q * pieces % 4 == 0:
                copies[2 + 2 * (q * pieces // 4)].wait()
                copies[3 + 2 * (q * pieces // 4)].wait()
            collected = jnp.zeros((16, LANES), jnp.float32)
            for e in range(16):
                d = 16 * q + e
                ends = []
                for half in range(2):
                    at = (2 * d + half) * LANES
                    section = lax.rem(at - bs * width + total, total)
                    beyond = lane + (section - pe)
                    wraps = (beyond >= 0) & (beyond < HALO)
                    cut = jnp.where(wraps, onward, tile(at))
                    out_ref[per * d + 8 * half : per * d + 8 * half + 8, :] = cut[:8]
                    out_ref[per * d + 16 + 4 * half : per * d + 20 + 4 * half, :] = cut[8:12]
                    ends.append(cut)
                both = jnp.where(lane < HALO, ends[0], ends[1])
                shift = (8 * e + HALO) % LANES
                both = pltpu.roll(both, shift, 1) if shift else both
                collected = jnp.where((lane >> 3) == e, both, collected)
            edges.append(collected)
        before = lax.rem(bs + parts - 1, parts)
        late = lax.rem(pe - HALO, LANES)
        tail_at = lax.rem(pe - HALO - late + bs * width, total)
        tail_next = lax.rem(tail_at + LANES, total)
        tail = jnp.where(lane >= late, tile(tail_at), tile(tail_next))
        tail = pltpu.roll(tail, lax.rem(8 * lax.rem(before, 16) - late + LANES, LANES), 1)
        skip = total - pe
        skip = jnp.where(skip < HALO, skip, 0)
        head = pltpu.roll(first, lax.rem(8 * lax.rem(bs, 16) + HALO - skip + LANES, LANES), 1)
        values = []
        for q in range(4):
            block = 16 * q + (lane >> 3)
            slot = lane & 7
            value = jnp.where((block == before) & (slot < HALO), tail, edges[q])
            values.append(jnp.where((block == bs) & (slot >= HALO), head, value))
        flat_ref[:, 0:64] = jnp.concatenate(values, axis=0).T
        parts_of = [jnp.zeros((16, LANES), jnp.float32)] * 4
        lane16 = lane[:16]
        for h in range(8):
            picked = flat_ref[pl.ds(h, 16, stride=8), :]
            for q in range(4):
                shift = (16 * h - 16 * q) % LANES
                moved = pltpu.roll(picked, shift, 1) if shift else picked
                parts_of[q] = jnp.where((lane16 >> 4) == h, moved, parts_of[q])
        flat = jnp.concatenate(parts_of, axis=0)
        lane = lax.broadcasted_iota(jnp.int32, (parts, LANES), 1)
        out_ref[pl.ds(per - 1, parts, stride=per), :] = jnp.where(
            lane < 64, pltpu.roll(flat, 1, 0), pltpu.roll(flat, parts - 1, 0)
        )

    smem = pl.BlockSpec(memory_space=pltpu.SMEM)
    vmem = pl.BlockSpec(memory_space=pltpu.VMEM)
    hbm = pl.BlockSpec(memory_space=pltpu.HBM)
    return pl.pallas_call(
        body,
        name="pack",
        out_shape=jax.ShapeDtypeStruct((parts * per, LANES), jnp.float32),
        in_specs=[smem, smem, hbm, hbm],
        out_specs=vmem,
        scratch_shapes=[
            pltpu.VMEM(state.shape, jnp.float32),
            pltpu.VMEM(inputs.shape, jnp.float32),
            pltpu.VMEM((rows_state, LANES), jnp.float32),
            pltpu.VMEM((rows_input, LANES), jnp.float32),
            pltpu.VMEM((LANES, LANES), jnp.float32),
            pltpu.SemaphoreType.DMA((2 + 2 * pieces,)),
        ],
        compiler_params=pltpu.CompilerParams(vmem_limit_bytes=32 << 20),
    )(
        block_start,
        period,
        pltpu.with_memory_space_constraint(state, pltpu.HBM),
        pltpu.with_memory_space_constraint(inputs, pltpu.HBM),
    )


def iterate(block_start, period, received, dynamics, gain, inverse, parts):
    states = dynamics.shape[0]
    controls = gain.shape[1]
    both = states + controls
    width = 2 * LANES
    rows = width + 2 * HALO
    span = states
    run = width // 8
    per = received.shape[0] // parts
    nt = (((1,), (1,)), ((), ()))
    nn = (((1,), (0,)), ((), ()))
    tn = (((0,), (0,)), ((), ()))

    def body(bs_ref, pe_ref, got_ref, a_ref, b_ref, k_ref, x_ref, u_ref, z_ref, sums_ref,
             nd_ref, ys_ref, vs_ref, gn_ref, ab_ref, *tiled):
        tiles = states // LANES
        neg_refs = tiled[: both // LANES]
        ws_refs = tiled[both // LANES : 2 * both // LANES]
        zs_refs = tiled[2 * both // LANES :]
        sub = lax.broadcasted_iota(jnp.int32, (8, LANES), 0)
        edge_row = lax.broadcasted_iota(jnp.int32, (8, states), 0)

        def lay(half, at, columns):
            for i in range(LANES // run):
                to = pl.ds(half * (LANES // run) + i, run, stride=8)
                neg_refs[at // LANES][to, :] = columns[run * i : run * i + run]

        def in_order(ref):
            return jnp.concatenate([ref[pl.ds(i, run, stride=8), :] for i in range(8)], axis=0)

        def keep_in(refs, values):
            for k, ref in enumerate(refs):
                ref[...] = values[:width, LANES * k : LANES * k + LANES]

        def joined(refs):
            return jnp.concatenate([ref[...] for ref in refs], axis=1)

        def back(values):
            near = pltpu.roll(values[width - 8 : width], 1, 0)
            halo = pltpu.roll(values[width:], 1, 0)
            begin = jnp.where(edge_row == 0, halo, near)
            return jnp.concatenate([begin, values[: width - 8], jnp.where(edge_row == 0, near, halo)], axis=0)

        def onward(values):
            near = pltpu.roll(values[:8], 7, 0)
            halo = pltpu.roll(values[width:], 7, 0)
            end = jnp.where(edge_row == 7, halo, near)
            return jnp.concatenate([values[8:width], end, jnp.where(edge_row == 7, near, halo)], axis=0)

        for g in range(states // LANES):
            for j in range(2):
                block = jnp.concatenate(
                    [got_ref[per * s + 8 * j : per * s + 8 * j + 8, :] for s in range(16 * g, 16 * g + 16)], axis=0
                )
                lay(j, LANES * g, -block.T)
        for g in range(controls // LANES):
            halves = ([], [])
            for s in range(32 * g, 32 * g + 32, 2):
                one = got_ref[per * s + 16 : per * s + 24, :]
                two = got_ref[per * (s + 1) + 16 : per * (s + 1) + 24, :]
                halves[0].append(jnp.where(sub < 4, one, pltpu.roll(two, 4, 0)))
                halves[1].append(jnp.where(sub < 4, pltpu.roll(one, 4, 0), two))
            for j in range(2):
                at = states + LANES * g
                lay(j, at, -jnp.concatenate(halves[j], axis=0).T)
        edge = got_ref[pl.ds(per - 1, parts, stride=per), :]
        high = edge.astype(jnp.bfloat16)
        rest = edge - high.astype(jnp.float32)
        middle = rest.astype(jnp.bfloat16)
        low = (rest - middle.astype(jnp.float32)).astype(jnp.bfloat16)
        cut = jnp.concatenate([high, middle, low], axis=0)
        src = lax.broadcasted_iota(jnp.int32, (3 * parts, both), 0) & (parts - 1)
        col = lax.broadcasted_iota(jnp.int32, (3 * parts, both), 1)
        owner = jnp.where(col < states, col >> 3, (col - states) >> 2)
        spread = jnp.where(owner == src, 1.0, 0.0).astype(jnp.bfloat16)
        wide = lax.dot_general(cut, spread, tn, preferred_element_type=jnp.float32)
        slot = lax.broadcasted_iota(jnp.int32, (LANES, both), 0) & 15
        col = lax.broadcasted_iota(jnp.int32, (LANES, both), 1)
        place = jnp.where(col < states, col & 7, 8 + (col & 3))
        wide = jnp.where(slot == place, wide, 0.0).reshape(8, 16, both).sum(axis=1)
        wide = -pltpu.roll(wide, HALO, 0)
        for k, ref in enumerate(neg_refs):
            ref[width : width + 8, :] = wide[:, LANES * k : LANES * k + LANES]

        ab_ref[:, :states] = a_ref[...]
        ab_ref[:, states:] = b_ref[...]
        for it in range(ITERS):
            last = it == ITERS - 1
            if it == 0:
                rhs = joined(neg_refs).astype(jnp.bfloat16)
            else:
                g = gn_ref[...]
                t = lax.dot_general(g, ab_ref[...], nn, preferred_element_type=jnp.float32)
                rhs = jnp.concatenate(
                    [
                        (nd_ref[...] + RHO * t[:, :states]).astype(jnp.bfloat16),
                        (joined(neg_refs[tiles:]) + RHO * t[:, states:]).astype(jnp.bfloat16),
                    ],
                    axis=1,
                )
            w = lax.dot_general(rhs, k_ref[...], nt, preferred_element_type=jnp.float32)
            wb = w.astype(jnp.bfloat16)
            primal, dual = 0.0, 0.0
            if last:
                idx = lax.rem(lax.axis_index("section") - bs_ref[0] + parts, parts)
                count = pe_ref[0] - idx * width
                row = lax.broadcasted_iota(jnp.int32, (width, span), 0)
                here = run * (row & 7) + (row >> 3) < count
                keep = lax.broadcasted_iota(jnp.int32, (LANES, width), 1) < count
                keep_in(ws_refs, w)
                for k in range(controls // LANES):
                    u_ref[LANES * k : LANES * k + LANES, :] = jnp.where(keep, in_order(ws_refs[tiles + k]).T, 0.0)
            for n in range(0, states, span):
                at = slice(n, n + span)
                x = w[:, at]
                pred = lax.dot_general(wb, ab_ref[at, :], nt, preferred_element_type=jnp.float32)
                if it == 0:
                    a, p = x, pred
                else:
                    a, p = x + ys_ref[:, at], pred + vs_ref[:, at]
                znew = 0.5 * (a + back(p))
                znn = onward(znew)
                if not last:
                    y = a - znew
                    v = p - znn
                    ys_ref[:, at] = y
                    vs_ref[:, at] = v
                    gn_ref[:, at] = (znn - v).astype(jnp.bfloat16)
                    nd_ref[:, at] = joined(neg_refs[:tiles]) + RHO * (znew - y)
                    if it == ITERS - 2:
                        keep_in(zs_refs, znew)
                else:
                    gap = (x - znew)[:width]
                    miss = (pred - znn)[:width]
                    step = znew[:width] - joined(zs_refs)
                    primal += jnp.sum(jnp.where(here, gap * gap + miss * miss, 0.0), axis=0, keepdims=True)
                    dual += RHO * RHO * jnp.sum(jnp.where(here, step * step, 0.0), axis=0, keepdims=True)
                    keep_in(zs_refs, znew)
                    for k in range(tiles):
                        to = slice(LANES * k, LANES * k + LANES)
                        x_ref[to, :] = jnp.where(keep, in_order(ws_refs[k]).T, 0.0)
                        z_ref[to, :] = jnp.where(keep, in_order(zs_refs[k]).T, 0.0)
            if last:
                lane = lax.broadcasted_iota(jnp.int32, (parts, LANES), 1)
                sums_ref[...] = jnp.where(lane == 0, jnp.sum(primal), jnp.where(lane == 1, jnp.sum(dual), 0.0))

    smem = pl.BlockSpec(memory_space=pltpu.SMEM)
    vmem = pl.BlockSpec(memory_space=pltpu.VMEM)
    return pl.pallas_call(
        body,
        name="iterate",
        out_shape=(
            pltpu.VMEM((states, width), jnp.float32),
            pltpu.VMEM((controls, width), jnp.float32),
            pltpu.VMEM((states, width), jnp.float32),
            pltpu.VMEM((parts, LANES), jnp.float32),
        ),
        in_specs=[smem, smem, vmem, vmem, vmem, vmem],
        out_specs=(vmem, vmem, vmem, vmem),
        scratch_shapes=[
            pltpu.VMEM((rows, states), jnp.float32),
            pltpu.VMEM((rows, states), jnp.float32),
            pltpu.VMEM((rows, states), jnp.float32),
            pltpu.VMEM((rows, states), jnp.bfloat16),
            pltpu.VMEM((states, both), jnp.bfloat16),
            *[pltpu.VMEM((rows, LANES), jnp.float32)] * (both // LANES),
            *[pltpu.VMEM((width, LANES), jnp.float32)] * ((both + states) // LANES),
        ],
        compiler_params=pltpu.CompilerParams(vmem_limit_bytes=48 << 20),
    )(block_start, period, received, dynamics, gain, inverse)


def swap(rows, parts):
    flat = rows.reshape(parts, 1, rows.size // parts)
    return lax.all_to_all(flat, "section", 0, 0, tiled=True)


def local(dynamics, gain, inverse, lin_state, lin_input, block_start, period):
    parts = lax.axis_size("section")
    packed = pack(block_start, period, lin_state, lin_input, parts)
    received = swap(packed, parts).reshape(packed.shape)
    x, u, z, sums = iterate(block_start, period, received, dynamics, gain, inverse, parts)
    sums = swap(sums, parts)
    return x, u, z, jnp.sqrt(jnp.sum(sums[:, 0, :2], axis=0))


def solution(mesh):
    return jax.shard_map(
        local,
        mesh=mesh,
        in_specs=(
            P("plant", None),
            P("plant", None),
            P("plant", None),
            P(("plant", "section"), None),
            P(("plant", "section"), None),
            P("plant"),
            P("plant"),
        ),
        out_specs=(P("plant", "section"), P("plant", "section"), P("plant", "section"), P("plant")),
        check_vma=False,
    )
```

```python
import jax
import jax.numpy as jnp
from jax import lax
from jax.experimental import pallas as pl
from jax.experimental.pallas import tpu as pltpu
from jax.sharding import PartitionSpec as P

ITERS = 4
RHO = 1.0
LANES = 128
HALO = 4


def pack(block_start, period, state, inputs, parts):
    rows_state, total = state.shape
    rows_input = inputs.shape[0]
    width = total // parts
    per = 2 * rows_state + 2 * rows_input + 1
    assert width == 2 * LANES and rows_state == 8 and rows_input == 4

    pieces = 2
    piece = total // pieces

    def body(bs_ref, pe_ref, st_hbm, in_hbm, out_ref, st_ref, in_ref, st_first, in_first, flat_ref, sems):
        bs = bs_ref[0]
        pe = pe_ref[0]
        opening = pl.ds(pl.multiple_of(bs * width, LANES), LANES)
        copies = [
            pltpu.make_async_copy(st_hbm.at[:, opening], st_first, sems.at[0]),
            pltpu.make_async_copy(in_hbm.at[:, opening], in_first, sems.at[1]),
        ]
        for q in range(pieces):
            at = slice(piece * q, piece * q + piece)
            copies.append(pltpu.make_async_copy(st_hbm.at[:, at], st_ref.at[:, at], sems.at[2 + 2 * q]))
            copies.append(pltpu.make_async_copy(in_hbm.at[:, at], in_ref.at[:, at], sems.at[3 + 2 * q]))
        for copy in copies:
            copy.start()
        lane = lax.broadcasted_iota(jnp.int32, (16, LANES), 1)
        spare = jnp.zeros((4, LANES), jnp.float32)

        def tile(position):
            at = pl.ds(pl.multiple_of(position, LANES), LANES)
            return jnp.concatenate([st_ref[:, at], in_ref[:, at], spare], axis=0)

        copies[0].wait()
        copies[1].wait()
        first = jnp.concatenate([st_first[...], in_first[...], spare], axis=0)
        onward = pltpu.roll(first, lax.rem(pe, LANES), 1)
        edges = []
        for q in range(4):
            if q * pieces % 4 == 0:
                copies[2 + 2 * (q * pieces // 4)].wait()
                copies[3 + 2 * (q * pieces // 4)].wait()
            collected = jnp.zeros((16, LANES), jnp.float32)
            for e in range(16):
                d = 16 * q + e
                ends = []
                for half in range(2):
                    at = (2 * d + half) * LANES
                    section = lax.rem(at - bs * width + total, total)
                    beyond = lane + (section - pe)
                    wraps = (beyond >= 0) & (beyond < HALO)
                    cut = jnp.where(wraps, onward, tile(at))
                    out_ref[per * d + 8 * half : per * d + 8 * half + 8, :] = cut[:8]
                    out_ref[per * d + 16 + 4 * half : per * d + 20 + 4 * half, :] = cut[8:12]
                    ends.append(cut)
                both = jnp.where(lane < HALO, ends[0], ends[1])
                shift = (8 * e + HALO) % LANES
                both = pltpu.roll(both, shift, 1) if shift else both
                collected = jnp.where((lane >> 3) == e, both, collected)
            edges.append(collected)
        before = lax.rem(bs + parts - 1, parts)
        late = lax.rem(pe - HALO, LANES)
        tail_at = lax.rem(pe - HALO - late + bs * width, total)
        tail_next = lax.rem(tail_at + LANES, total)
        tail = jnp.where(lane >= late, tile(tail_at), tile(tail_next))
        tail = pltpu.roll(tail, lax.rem(8 * lax.rem(before, 16) - late + LANES, LANES), 1)
        skip = total - pe
        skip = jnp.where(skip < HALO, skip, 0)
        head = pltpu.roll(first, lax.rem(8 * lax.rem(bs, 16) + HALO - skip + LANES, LANES), 1)
        values = []
        for q in range(4):
            block = 16 * q + (lane >> 3)
            slot = lane & 7
            value = jnp.where((block == before) & (slot < HALO), tail, edges[q])
            values.append(jnp.where((block == bs) & (slot >= HALO), head, value))
        flat_ref[:, 0:64] = jnp.concatenate(values, axis=0).T
        parts_of = [jnp.zeros((16, LANES), jnp.float32)] * 4
        lane16 = lane[:16]
        for h in range(8):
            picked = flat_ref[pl.ds(h, 16, stride=8), :]
            for q in range(4):
                shift = (16 * h - 16 * q) % LANES
                moved = pltpu.roll(picked, shift, 1) if shift else picked
                parts_of[q] = jnp.where((lane16 >> 4) == h, moved, parts_of[q])
        flat = jnp.concatenate(parts_of, axis=0)
        lane = lax.broadcasted_iota(jnp.int32, (parts, LANES), 1)
        out_ref[pl.ds(per - 1, parts, stride=per), :] = jnp.where(
            lane < 64, pltpu.roll(flat, 1, 0), pltpu.roll(flat, parts - 1, 0)
        )

    smem = pl.BlockSpec(memory_space=pltpu.SMEM)
    vmem = pl.BlockSpec(memory_space=pltpu.VMEM)
    hbm = pl.BlockSpec(memory_space=pltpu.HBM)
    return pl.pallas_call(
        body,
        name="pack",
        out_shape=jax.ShapeDtypeStruct((parts * per, LANES), jnp.float32),
        in_specs=[smem, smem, hbm, hbm],
        out_specs=vmem,
        scratch_shapes=[
            pltpu.VMEM(state.shape, jnp.float32),
            pltpu.VMEM(inputs.shape, jnp.float32),
            pltpu.VMEM((rows_state, LANES), jnp.float32),
            pltpu.VMEM((rows_input, LANES), jnp.float32),
            pltpu.VMEM((LANES, LANES), jnp.float32),
            pltpu.SemaphoreType.DMA((2 + 2 * pieces,)),
        ],
        compiler_params=pltpu.CompilerParams(vmem_limit_bytes=32 << 20),
    )(
        block_start,
        period,
        pltpu.with_memory_space_constraint(state, pltpu.HBM),
        pltpu.with_memory_space_constraint(inputs, pltpu.HBM),
    )


def iterate(block_start, period, received, dynamics, gain, inverse, parts):
    states = dynamics.shape[0]
    controls = gain.shape[1]
    both = states + controls
    width = 2 * LANES
    rows = width + 2 * HALO
    span = states
    run = width // 8
    per = received.shape[0] // parts
    nt = (((1,), (1,)), ((), ()))
    nn = (((1,), (0,)), ((), ()))
    tn = (((0,), (0,)), ((), ()))

    def body(bs_ref, pe_ref, got_ref, a_ref, b_ref, k_ref, x_ref, u_ref, z_ref, sums_ref,
             nd_ref, ys_ref, vs_ref, gn_ref, ab_ref, *tiled):
        tiles = states // LANES
        neg_refs = tiled[: both // LANES]
        ws_refs = tiled[both // LANES : 2 * both // LANES]
        zs_refs = tiled[2 * both // LANES :]
        sub = lax.broadcasted_iota(jnp.int32, (8, LANES), 0)
        edge_row = lax.broadcasted_iota(jnp.int32, (8, states), 0)

        def lay(half, at, columns):
            for i in range(LANES // run):
                to = pl.ds(half * (LANES // run) + i, run, stride=8)
                neg_refs[at // LANES][to, :] = columns[run * i : run * i + run]

        def in_order(ref):
            return jnp.concatenate([ref[pl.ds(i, run, stride=8), :] for i in range(8)], axis=0)

        def keep_in(refs, values):
            for k, ref in enumerate(refs):
                ref[...] = values[:width, LANES * k : LANES * k + LANES]

        def joined(refs):
            return jnp.concatenate([ref[...] for ref in refs], axis=1)

        def back(values):
            near = pltpu.roll(values[width - 8 : width], 1, 0)
            halo = pltpu.roll(values[width:], 1, 0)
            begin = jnp.where(edge_row == 0, halo, near)
            return jnp.concatenate([begin, values[: width - 8], jnp.where(edge_row == 0, near, halo)], axis=0)

        def onward(values):
            near = pltpu.roll(values[:8], 7, 0)
            halo = pltpu.roll(values[width:], 7, 0)
            end = jnp.where(edge_row == 7, halo, near)
            return jnp.concatenate([values[8:width], end, jnp.where(edge_row == 7, near, halo)], axis=0)

        for g in range(states // LANES):
            for j in range(2):
                block = jnp.concatenate(
                    [got_ref[per * s + 8 * j : per * s + 8 * j + 8, :] for s in range(16 * g, 16 * g + 16)], axis=0
                )
                lay(j, LANES * g, -block.T)
        for g in range(controls // LANES):
            halves = ([], [])
            for s in range(32 * g, 32 * g + 32, 2):
                one = got_ref[per * s + 16 : per * s + 24, :]
                two = got_ref[per * (s + 1) + 16 : per * (s + 1) + 24, :]
                halves[0].append(jnp.where(sub < 4, one, pltpu.roll(two, 4, 0)))
                halves[1].append(jnp.where(sub < 4, pltpu.roll(one, 4, 0), two))
            for j in range(2):
                at = states + LANES * g
                lay(j, at, -jnp.concatenate(halves[j], axis=0).T)
        edge = got_ref[pl.ds(per - 1, parts, stride=per), :]
        high = edge.astype(jnp.bfloat16)
        rest = edge - high.astype(jnp.float32)
        middle = rest.astype(jnp.bfloat16)
        low = (rest - middle.astype(jnp.float32)).astype(jnp.bfloat16)
        cut = jnp.concatenate([high, middle, low], axis=0)
        src = lax.broadcasted_iota(jnp.int32, (3 * parts, both), 0) & (parts - 1)
        col = lax.broadcasted_iota(jnp.int32, (3 * parts, both), 1)
        owner = jnp.where(col < states, col >> 3, (col - states) >> 2)
        spread = jnp.where(owner == src, 1.0, 0.0).astype(jnp.bfloat16)
        wide = lax.dot_general(cut, spread, tn, preferred_element_type=jnp.float32)
        slot = lax.broadcasted_iota(jnp.int32, (LANES, both), 0) & 15
        col = lax.broadcasted_iota(jnp.int32, (LANES, both), 1)
        place = jnp.where(col < states, col & 7, 8 + (col & 3))
        wide = jnp.where(slot == place, wide, 0.0).reshape(8, 16, both).sum(axis=1)
        wide = -pltpu.roll(wide, HALO, 0)
        for k, ref in enumerate(neg_refs):
            ref[width : width + 8, :] = wide[:, LANES * k : LANES * k + LANES]

        ab_ref[:, :states] = a_ref[...]
        ab_ref[:, states:] = b_ref[...]
        for it in range(ITERS):
            last = it == ITERS - 1
            if it == 0:
                rhs = joined(neg_refs).astype(jnp.bfloat16)
            else:
                g = gn_ref[...]
                t = lax.dot_general(g, ab_ref[...], nn, preferred_element_type=jnp.float32)
                rhs = jnp.concatenate(
                    [
                        (nd_ref[...] + RHO * t[:, :states]).astype(jnp.bfloat16),
                        (joined(neg_refs[tiles:]) + RHO * t[:, states:]).astype(jnp.bfloat16),
                    ],
                    axis=1,
                )
            w = lax.dot_general(rhs, k_ref[...], nt, preferred_element_type=jnp.float32)
            wb = w.astype(jnp.bfloat16)
            primal, dual = 0.0, 0.0
            if last:
                idx = lax.rem(lax.axis_index("section") - bs_ref[0] + parts, parts)
                count = pe_ref[0] - idx * width
                row = lax.broadcasted_iota(jnp.int32, (width, span), 0)
                here = run * (row & 7) + (row >> 3) < count
                keep = lax.broadcasted_iota(jnp.int32, (LANES, width), 1) < count
                keep_in(ws_refs, w)
                for k in range(controls // LANES):
                    u_ref[LANES * k : LANES * k + LANES, :] = jnp.where(keep, in_order(ws_refs[tiles + k]).T, 0.0)
            for n in range(0, states, span):
                at = slice(n, n + span)
                x = w[:, at]
                pred = lax.dot_general(wb, ab_ref[at, :], nt, preferred_element_type=jnp.float32)
                if it == 0:
                    a, p = x, pred
                else:
                    a, p = x + ys_ref[:, at], pred + vs_ref[:, at]
                znew = 0.5 * (a + back(p))
                znn = onward(znew)
                if not last:
                    y = a - znew
                    v = p - znn
                    ys_ref[:, at] = y
                    vs_ref[:, at] = v
                    gn_ref[:, at] = (znn - v).astype(jnp.bfloat16)
                    nd_ref[:, at] = joined(neg_refs[:tiles]) + RHO * (znew - y)
                    if it == ITERS - 2:
                        keep_in(zs_refs, znew)
                else:
                    gap = (x - znew)[:width]
                    miss = (pred - znn)[:width]
                    step = znew[:width] - joined(zs_refs)
                    primal += jnp.sum(jnp.where(here, gap * gap + miss * miss, 0.0), axis=0, keepdims=True)
                    dual += RHO * RHO * jnp.sum(jnp.where(here, step * step, 0.0), axis=0, keepdims=True)
                    keep_in(zs_refs, znew)
                    for k in range(tiles):
                        to = slice(LANES * k, LANES * k + LANES)
                        x_ref[to, :] = jnp.where(keep, in_order(ws_refs[k]).T, 0.0)
                        z_ref[to, :] = jnp.where(keep, in_order(zs_refs[k]).T, 0.0)
            if last:
                lane = lax.broadcasted_iota(jnp.int32, (parts, LANES), 1)
                sums_ref[...] = jnp.where(lane == 0, jnp.sum(primal), jnp.where(lane == 1, jnp.sum(dual), 0.0))

    smem = pl.BlockSpec(memory_space=pltpu.SMEM)
    vmem = pl.BlockSpec(memory_space=pltpu.VMEM)
    return pl.pallas_call(
        body,
        name="iterate",
        out_shape=(
            pltpu.VMEM((states, width), jnp.float32),
            pltpu.VMEM((controls, width), jnp.float32),
            pltpu.VMEM((states, width), jnp.float32),
            jax.ShapeDtypeStruct((parts, LANES), jnp.float32),
        ),
        in_specs=[smem, smem, vmem, vmem, vmem, vmem],
        out_specs=(vmem, vmem, vmem, vmem),
        scratch_shapes=[
            pltpu.VMEM((rows, states), jnp.float32),
            pltpu.VMEM((rows, states), jnp.float32),
            pltpu.VMEM((rows, states), jnp.float32),
            pltpu.VMEM((rows, states), jnp.bfloat16),
            pltpu.VMEM((states, both), jnp.bfloat16),
            *[pltpu.VMEM((rows, LANES), jnp.float32)] * (both // LANES),
            *[pltpu.VMEM((width, LANES), jnp.float32)] * ((both + states) // LANES),
        ],
        compiler_params=pltpu.CompilerParams(vmem_limit_bytes=48 << 20),
    )(block_start, period, received, dynamics, gain, inverse)


def finish(sums, *blocks):
    def body(sums_ref, *refs):
        sources, sinks = refs[: len(blocks)], refs[len(blocks) : 2 * len(blocks)]
        norms_ref, sems = refs[-2:]
        copies = [pltpu.make_async_copy(a, b, sems.at[i]) for i, (a, b) in enumerate(zip(sources, sinks))]
        for copy in copies:
            copy.start()
        norms_ref[...] = jnp.sqrt(jnp.sum(sums_ref[...], axis=0, keepdims=True))[:, :2]
        for copy in copies:
            copy.wait()

    vmem = pl.BlockSpec(memory_space=pltpu.VMEM)
    hbm = pl.BlockSpec(memory_space=pltpu.HBM)
    return pl.pallas_call(
        body,
        name="finish",
        out_shape=(
            *[pltpu.HBM(b.shape, b.dtype) for b in blocks],
            jax.ShapeDtypeStruct((1, 2), jnp.float32),
        ),
        in_specs=[vmem] * (1 + len(blocks)),
        out_specs=(*[hbm] * len(blocks), vmem),
        scratch_shapes=[pltpu.SemaphoreType.DMA((len(blocks),))],
    )(*[pltpu.with_memory_space_constraint(b, pltpu.VMEM) for b in (sums, *blocks)])


def swap(rows, parts):
    flat = rows.reshape(parts, 1, rows.size // parts)
    return lax.all_to_all(flat, "section", 0, 0, tiled=True)


def local(dynamics, gain, inverse, lin_state, lin_input, block_start, period):
    parts = lax.axis_size("section")
    packed = pack(block_start, period, lin_state, lin_input, parts)
    received = swap(packed, parts).reshape(packed.shape)
    x, u, z, sums = iterate(block_start, period, received, dynamics, gain, inverse, parts)
    sums = swap(sums, parts).reshape(sums.shape)
    x, u, z, norms = finish(sums, x, u, z)
    return x, u, z, norms.reshape(2)


def solution(mesh):
    return jax.shard_map(
        local,
        mesh=mesh,
        in_specs=(
            P("plant", None),
            P("plant", None),
            P("plant", None),
            P(("plant", "section"), None),
            P(("plant", "section"), None),
            P("plant"),
            P("plant"),
        ),
        out_specs=(P("plant", "section"), P("plant", "section"), P("plant", "section"), P("plant")),
        check_vma=False,
    )
```

```python
import jax
import jax.numpy as jnp
from jax import lax
from jax.experimental import pallas as pl
from jax.experimental.pallas import tpu as pltpu
from jax.sharding import PartitionSpec as P

ITERS = 4
RHO = 1.0
LANES = 128
HALO = 4


def pack(block_start, period, state, inputs, parts):
    rows_state, total = state.shape
    rows_input = inputs.shape[0]
    width = total // parts
    per = 2 * rows_state + 2 * rows_input + 1
    assert width == 2 * LANES and rows_state == 8 and rows_input == 4

    pieces = 2
    piece = total // pieces

    def body(bs_ref, pe_ref, st_hbm, in_hbm, out_ref, st_ref, in_ref, st_first, in_first, flat_ref, sems):
        bs = bs_ref[0]
        pe = pe_ref[0]
        opening = pl.ds(pl.multiple_of(bs * width, LANES), LANES)
        copies = [
            pltpu.make_async_copy(st_hbm.at[:, opening], st_first, sems.at[0]),
            pltpu.make_async_copy(in_hbm.at[:, opening], in_first, sems.at[1]),
        ]
        for q in range(pieces):
            at = slice(piece * q, piece * q + piece)
            copies.append(pltpu.make_async_copy(st_hbm.at[:, at], st_ref.at[:, at], sems.at[2 + 2 * q]))
            copies.append(pltpu.make_async_copy(in_hbm.at[:, at], in_ref.at[:, at], sems.at[3 + 2 * q]))
        for copy in copies:
            copy.start()
        lane = lax.broadcasted_iota(jnp.int32, (16, LANES), 1)
        spare = jnp.zeros((4, LANES), jnp.float32)

        def tile(position):
            at = pl.ds(pl.multiple_of(position, LANES), LANES)
            return jnp.concatenate([st_ref[:, at], in_ref[:, at], spare], axis=0)

        copies[0].wait()
        copies[1].wait()
        first = jnp.concatenate([st_first[...], in_first[...], spare], axis=0)
        onward = pltpu.roll(first, lax.rem(pe, LANES), 1)
        edges = []
        for q in range(4):
            if q * pieces % 4 == 0:
                copies[2 + 2 * (q * pieces // 4)].wait()
                copies[3 + 2 * (q * pieces // 4)].wait()
            collected = jnp.zeros((16, LANES), jnp.float32)
            for e in range(16):
                d = 16 * q + e
                ends = []
                for half in range(2):
                    at = (2 * d + half) * LANES
                    section = lax.rem(at - bs * width + total, total)
                    beyond = lane + (section - pe)
                    wraps = (beyond >= 0) & (beyond < HALO)
                    cut = jnp.where(wraps, onward, tile(at))
                    out_ref[per * d + 8 * half : per * d + 8 * half + 8, :] = cut[:8]
                    out_ref[per * d + 16 + 4 * half : per * d + 20 + 4 * half, :] = cut[8:12]
                    ends.append(cut)
                both = jnp.where(lane < HALO, ends[0], ends[1])
                shift = (8 * e + HALO) % LANES
                both = pltpu.roll(both, shift, 1) if shift else both
                collected = jnp.where((lane >> 3) == e, both, collected)
            edges.append(collected)
        before = lax.rem(bs + parts - 1, parts)
        late = lax.rem(pe - HALO, LANES)
        tail_at = lax.rem(pe - HALO - late + bs * width, total)
        tail_next = lax.rem(tail_at + LANES, total)
        tail = jnp.where(lane >= late, tile(tail_at), tile(tail_next))
        tail = pltpu.roll(tail, lax.rem(8 * lax.rem(before, 16) - late + LANES, LANES), 1)
        skip = total - pe
        skip = jnp.where(skip < HALO, skip, 0)
        head = pltpu.roll(first, lax.rem(8 * lax.rem(bs, 16) + HALO - skip + LANES, LANES), 1)
        values = []
        for q in range(4):
            block = 16 * q + (lane >> 3)
            slot = lane & 7
            value = jnp.where((block == before) & (slot < HALO), tail, edges[q])
            values.append(jnp.where((block == bs) & (slot >= HALO), head, value))
        flat_ref[:, 0:64] = jnp.concatenate(values, axis=0).T
        parts_of = [jnp.zeros((16, LANES), jnp.float32)] * 4
        lane16 = lane[:16]
        for h in range(8):
            picked = flat_ref[pl.ds(h, 16, stride=8), :]
            for q in range(4):
                shift = (16 * h - 16 * q) % LANES
                moved = pltpu.roll(picked, shift, 1) if shift else picked
                parts_of[q] = jnp.where((lane16 >> 4) == h, moved, parts_of[q])
        flat = jnp.concatenate(parts_of, axis=0)
        lane = lax.broadcasted_iota(jnp.int32, (parts, LANES), 1)
        out_ref[pl.ds(per - 1, parts, stride=per), :] = jnp.where(
            lane < 64, pltpu.roll(flat, 1, 0), pltpu.roll(flat, parts - 1, 0)
        )

    smem = pl.BlockSpec(memory_space=pltpu.SMEM)
    vmem = pl.BlockSpec(memory_space=pltpu.VMEM)
    hbm = pl.BlockSpec(memory_space=pltpu.HBM)
    return pl.pallas_call(
        body,
        name="pack",
        out_shape=jax.ShapeDtypeStruct((parts * per, LANES), jnp.float32),
        in_specs=[smem, smem, hbm, hbm],
        out_specs=vmem,
        scratch_shapes=[
            pltpu.VMEM(state.shape, jnp.float32),
            pltpu.VMEM(inputs.shape, jnp.float32),
            pltpu.VMEM((rows_state, LANES), jnp.float32),
            pltpu.VMEM((rows_input, LANES), jnp.float32),
            pltpu.VMEM((LANES, LANES), jnp.float32),
            pltpu.SemaphoreType.DMA((2 + 2 * pieces,)),
        ],
        compiler_params=pltpu.CompilerParams(vmem_limit_bytes=32 << 20),
    )(
        block_start,
        period,
        pltpu.with_memory_space_constraint(state, pltpu.HBM),
        pltpu.with_memory_space_constraint(inputs, pltpu.HBM),
    )


def iterate(block_start, period, received, dynamics, gain, inverse, parts):
    states = dynamics.shape[0]
    controls = gain.shape[1]
    both = states + controls
    width = 2 * LANES
    rows = width + 2 * HALO
    span = states
    run = width // 8
    per = received.shape[0] // parts
    nt = (((1,), (1,)), ((), ()))
    nn = (((1,), (0,)), ((), ()))
    tn = (((0,), (0,)), ((), ()))

    def body(bs_ref, pe_ref, got_ref, a_ref, b_ref, k_ref, x_ref, u_ref, z_ref, sums_ref,
             nd_ref, ys_ref, vs_ref, gn_ref, ab_ref, *tiled):
        tiles = states // LANES
        neg_refs = tiled[: both // LANES]
        ws_refs = tiled[both // LANES : 2 * both // LANES]
        zs_refs = tiled[2 * both // LANES :]
        sub = lax.broadcasted_iota(jnp.int32, (8, LANES), 0)
        edge_row = lax.broadcasted_iota(jnp.int32, (8, states), 0)

        def lay(half, at, columns):
            for i in range(LANES // run):
                to = pl.ds(half * (LANES // run) + i, run, stride=8)
                neg_refs[at // LANES][to, :] = columns[run * i : run * i + run]

        def in_order(ref):
            return jnp.concatenate([ref[pl.ds(i, run, stride=8), :] for i in range(8)], axis=0)

        def keep_in(refs, values):
            for k, ref in enumerate(refs):
                ref[...] = values[:width, LANES * k : LANES * k + LANES]

        def joined(refs):
            return jnp.concatenate([ref[...] for ref in refs], axis=1)

        def back(values):
            near = pltpu.roll(values[width - 8 : width], 1, 0)
            halo = pltpu.roll(values[width:], 1, 0)
            begin = jnp.where(edge_row == 0, halo, near)
            return jnp.concatenate([begin, values[: width - 8], jnp.where(edge_row == 0, near, halo)], axis=0)

        def onward(values):
            near = pltpu.roll(values[:8], 7, 0)
            halo = pltpu.roll(values[width:], 7, 0)
            end = jnp.where(edge_row == 7, halo, near)
            return jnp.concatenate([values[8:width], end, jnp.where(edge_row == 7, near, halo)], axis=0)

        for g in range(states // LANES):
            for j in range(2):
                block = jnp.concatenate(
                    [got_ref[per * s + 8 * j : per * s + 8 * j + 8, :] for s in range(16 * g, 16 * g + 16)], axis=0
                )
                lay(j, LANES * g, -block.T)
        for g in range(controls // LANES):
            halves = ([], [])
            for s in range(32 * g, 32 * g + 32, 2):
                one = got_ref[per * s + 16 : per * s + 24, :]
                two = got_ref[per * (s + 1) + 16 : per * (s + 1) + 24, :]
                halves[0].append(jnp.where(sub < 4, one, pltpu.roll(two, 4, 0)))
                halves[1].append(jnp.where(sub < 4, pltpu.roll(one, 4, 0), two))
            for j in range(2):
                at = states + LANES * g
                lay(j, at, -jnp.concatenate(halves[j], axis=0).T)
        edge = got_ref[pl.ds(per - 1, parts, stride=per), :]
        high = edge.astype(jnp.bfloat16)
        rest = edge - high.astype(jnp.float32)
        middle = rest.astype(jnp.bfloat16)
        low = (rest - middle.astype(jnp.float32)).astype(jnp.bfloat16)
        cut = jnp.concatenate([high, middle, low], axis=0)
        src = lax.broadcasted_iota(jnp.int32, (3 * parts, both), 0) & (parts - 1)
        col = lax.broadcasted_iota(jnp.int32, (3 * parts, both), 1)
        owner = jnp.where(col < states, col >> 3, (col - states) >> 2)
        spread = jnp.where(owner == src, 1.0, 0.0).astype(jnp.bfloat16)
        wide = lax.dot_general(cut, spread, tn, preferred_element_type=jnp.float32)
        slot = lax.broadcasted_iota(jnp.int32, (LANES, both), 0) & 15
        col = lax.broadcasted_iota(jnp.int32, (LANES, both), 1)
        place = jnp.where(col < states, col & 7, 8 + (col & 3))
        wide = jnp.where(slot == place, wide, 0.0).reshape(8, 16, both).sum(axis=1)
        wide = -pltpu.roll(wide, HALO, 0)
        for k, ref in enumerate(neg_refs):
            ref[width : width + 8, :] = wide[:, LANES * k : LANES * k + LANES]

        ab_ref[:, :states] = a_ref[...]
        ab_ref[:, states:] = b_ref[...]
        for it in range(ITERS):
            last = it == ITERS - 1
            if it == 0:
                rhs = joined(neg_refs).astype(jnp.bfloat16)
            else:
                g = gn_ref[...]
                t = lax.dot_general(g, ab_ref[...], nn, preferred_element_type=jnp.float32)
                rhs = jnp.concatenate(
                    [
                        (nd_ref[...] + RHO * t[:, :states]).astype(jnp.bfloat16),
                        (joined(neg_refs[tiles:]) + RHO * t[:, states:]).astype(jnp.bfloat16),
                    ],
                    axis=1,
                )
            w = lax.dot_general(rhs, k_ref[...], nt, preferred_element_type=jnp.float32)
            wb = w.astype(jnp.bfloat16)
            primal, dual = 0.0, 0.0
            if last:
                idx = lax.rem(lax.axis_index("section") - bs_ref[0] + parts, parts)
                count = pe_ref[0] - idx * width
                row = lax.broadcasted_iota(jnp.int32, (width, span), 0)
                here = run * (row & 7) + (row >> 3) < count
                keep = lax.broadcasted_iota(jnp.int32, (LANES, width), 1) < count
                keep_in(ws_refs, w)
                for k in range(controls // LANES):
                    u_ref[LANES * k : LANES * k + LANES, :] = jnp.where(keep, in_order(ws_refs[tiles + k]).T, 0.0)
            for n in range(0, states, span):
                at = slice(n, n + span)
                x = w[:, at]
                pred = lax.dot_general(wb, ab_ref[at, :], nt, preferred_element_type=jnp.float32)
                if it == 0:
                    a, p = x, pred
                else:
                    a, p = x + ys_ref[:, at], pred + vs_ref[:, at]
                znew = 0.5 * (a + back(p))
                znn = onward(znew)
                if not last:
                    y = a - znew
                    v = p - znn
                    ys_ref[:, at] = y
                    vs_ref[:, at] = v
                    gn_ref[:, at] = (znn - v).astype(jnp.bfloat16)
                    nd_ref[:, at] = joined(neg_refs[:tiles]) + RHO * (znew - y)
                    if it == ITERS - 2:
                        keep_in(zs_refs, znew)
                else:
                    gap = (x - znew)[:width]
                    miss = (pred - znn)[:width]
                    step = znew[:width] - joined(zs_refs)
                    primal += jnp.sum(jnp.where(here, gap * gap + miss * miss, 0.0), axis=0, keepdims=True)
                    dual += RHO * RHO * jnp.sum(jnp.where(here, step * step, 0.0), axis=0, keepdims=True)
                    keep_in(zs_refs, znew)
                    for k in range(tiles):
                        to = slice(LANES * k, LANES * k + LANES)
                        x_ref[to, :] = jnp.where(keep, in_order(ws_refs[k]).T, 0.0)
                        z_ref[to, :] = jnp.where(keep, in_order(zs_refs[k]).T, 0.0)
            if last:
                lane = lax.broadcasted_iota(jnp.int32, (parts, LANES), 1)
                sums_ref[...] = jnp.where(lane == 0, jnp.sum(primal), jnp.where(lane == 1, jnp.sum(dual), 0.0))

    smem = pl.BlockSpec(memory_space=pltpu.SMEM)
    vmem = pl.BlockSpec(memory_space=pltpu.VMEM)
    return pl.pallas_call(
        body,
        name="iterate",
        out_shape=(
            pltpu.VMEM((states, width), jnp.float32),
            pltpu.VMEM((controls, width), jnp.float32),
            pltpu.VMEM((states, width), jnp.float32),
            jax.ShapeDtypeStruct((parts, LANES), jnp.float32),
        ),
        in_specs=[smem, smem, vmem, vmem, vmem, vmem],
        out_specs=(vmem, vmem, vmem, vmem),
        scratch_shapes=[
            pltpu.VMEM((rows, states), jnp.float32),
            pltpu.VMEM((rows, states), jnp.float32),
            pltpu.VMEM((rows, states), jnp.float32),
            pltpu.VMEM((rows, states), jnp.bfloat16),
            pltpu.VMEM((states, both), jnp.bfloat16),
            *[pltpu.VMEM((rows, LANES), jnp.float32)] * (both // LANES),
            *[pltpu.VMEM((width, LANES), jnp.float32)] * ((both + states) // LANES),
        ],
        compiler_params=pltpu.CompilerParams(vmem_limit_bytes=48 << 20),
    )(block_start, period, received, dynamics, gain, inverse)


def finish(sums, *blocks):
    def body(sums_ref, *refs):
        sources, sinks = refs[: len(blocks)], refs[len(blocks) : 2 * len(blocks)]
        norms_hbm, norms_ref, sems = refs[-3:]
        copies = [pltpu.make_async_copy(a, b, sems.at[i]) for i, (a, b) in enumerate(zip(sources, sinks))]
        for copy in copies:
            copy.start()
        norms_ref[...] = jnp.sqrt(jnp.sum(sums_ref[...], axis=0, keepdims=True))[:, :2]
        copies.append(pltpu.make_async_copy(norms_ref, norms_hbm, sems.at[len(blocks)]))
        copies[-1].start()
        for copy in copies:
            copy.wait()

    vmem = pl.BlockSpec(memory_space=pltpu.VMEM)
    hbm = pl.BlockSpec(memory_space=pltpu.HBM)
    return pl.pallas_call(
        body,
        name="finish",
        out_shape=(
            *[pltpu.HBM(b.shape, b.dtype) for b in blocks],
            pltpu.HBM((1, 2), jnp.float32),
        ),
        in_specs=[vmem] * (1 + len(blocks)),
        out_specs=(*[hbm] * len(blocks), hbm),
        scratch_shapes=[pltpu.VMEM((1, 2), jnp.float32), pltpu.SemaphoreType.DMA((len(blocks) + 1,))],
    )(*[pltpu.with_memory_space_constraint(b, pltpu.VMEM) for b in (sums, *blocks)])


def swap(rows, parts):
    flat = rows.reshape(parts, 1, rows.size // parts)
    return lax.all_to_all(flat, "section", 0, 0, tiled=True)


def local(dynamics, gain, inverse, lin_state, lin_input, block_start, period):
    parts = lax.axis_size("section")
    packed = pack(block_start, period, lin_state, lin_input, parts)
    received = swap(packed, parts).reshape(packed.shape)
    x, u, z, sums = iterate(block_start, period, received, dynamics, gain, inverse, parts)
    sums = swap(sums, parts).reshape(sums.shape)
    x, u, z, norms = finish(sums, x, u, z)
    return x, u, z, norms.reshape(2)


def solution(mesh):
    return jax.shard_map(
        local,
        mesh=mesh,
        in_specs=(
            P("plant", None),
            P("plant", None),
            P("plant", None),
            P(("plant", "section"), None),
            P(("plant", "section"), None),
            P("plant"),
            P("plant"),
        ),
        out_specs=(P("plant", "section"), P("plant", "section"), P("plant", "section"), P("plant")),
        check_vma=False,
    )
```

```python
import jax
import jax.numpy as jnp
from jax import lax
from jax.experimental import pallas as pl
from jax.experimental.pallas import tpu as pltpu
from jax.sharding import PartitionSpec as P

ITERS = 4
RHO = 1.0
LANES = 128
HALO = 4


def pack(block_start, period, state, inputs, parts):
    rows_state, total = state.shape
    rows_input = inputs.shape[0]
    width = total // parts
    per = 2 * rows_state + 2 * rows_input + 1
    assert width == 2 * LANES and rows_state == 8 and rows_input == 4

    pieces = 1
    piece = total // pieces

    def body(bs_hbm, pe_hbm, st_hbm, in_hbm, out_ref, bs_ref, pe_ref, st_ref, in_ref, flat_ref, sems):
        copies = [
            pltpu.make_async_copy(bs_hbm, bs_ref, sems.at[0]),
            pltpu.make_async_copy(pe_hbm, pe_ref, sems.at[1]),
        ]
        for q in range(pieces):
            at = slice(piece * q, piece * q + piece)
            copies.append(pltpu.make_async_copy(st_hbm.at[:, at], st_ref.at[:, at], sems.at[2 + 2 * q]))
            copies.append(pltpu.make_async_copy(in_hbm.at[:, at], in_ref.at[:, at], sems.at[3 + 2 * q]))
        for copy in copies:
            copy.start()
        lane = lax.broadcasted_iota(jnp.int32, (16, LANES), 1)
        spare = jnp.zeros((4, LANES), jnp.float32)

        def tile(position):
            at = pl.ds(pl.multiple_of(position, LANES), LANES)
            return jnp.concatenate([st_ref[:, at], in_ref[:, at], spare], axis=0)

        copies[0].wait()
        copies[1].wait()
        bs = bs_ref[0, 0]
        pe = pe_ref[0, 0]
        for copy in copies[2:]:
            copy.wait()
        first = tile(bs * width)
        onward = pltpu.roll(first, lax.rem(pe, LANES), 1)
        edges = []
        for q in range(4):
            collected = jnp.zeros((16, LANES), jnp.float32)
            for e in range(16):
                d = 16 * q + e
                ends = []
                for half in range(2):
                    at = (2 * d + half) * LANES
                    section = lax.rem(at - bs * width + total, total)
                    beyond = lane + (section - pe)
                    wraps = (beyond >= 0) & (beyond < HALO)
                    cut = jnp.where(wraps, onward, tile(at))
                    out_ref[per * d + 8 * half : per * d + 8 * half + 8, :] = cut[:8]
                    out_ref[per * d + 16 + 4 * half : per * d + 20 + 4 * half, :] = cut[8:12]
                    ends.append(cut)
                both = jnp.where(lane < HALO, ends[0], ends[1])
                shift = (8 * e + HALO) % LANES
                both = pltpu.roll(both, shift, 1) if shift else both
                collected = jnp.where((lane >> 3) == e, both, collected)
            edges.append(collected)
        before = lax.rem(bs + parts - 1, parts)
        late = lax.rem(pe - HALO, LANES)
        tail_at = lax.rem(pe - HALO - late + bs * width, total)
        tail_next = lax.rem(tail_at + LANES, total)
        tail = jnp.where(lane >= late, tile(tail_at), tile(tail_next))
        tail = pltpu.roll(tail, lax.rem(8 * lax.rem(before, 16) - late + LANES, LANES), 1)
        skip = total - pe
        skip = jnp.where(skip < HALO, skip, 0)
        head = pltpu.roll(first, lax.rem(8 * lax.rem(bs, 16) + HALO - skip + LANES, LANES), 1)
        values = []
        for q in range(4):
            block = 16 * q + (lane >> 3)
            slot = lane & 7
            value = jnp.where((block == before) & (slot < HALO), tail, edges[q])
            values.append(jnp.where((block == bs) & (slot >= HALO), head, value))
        flat_ref[:, 0:64] = jnp.concatenate(values, axis=0).T
        parts_of = [jnp.zeros((16, LANES), jnp.float32)] * 4
        lane16 = lane[:16]
        for h in range(8):
            picked = flat_ref[pl.ds(h, 16, stride=8), :]
            for q in range(4):
                shift = (16 * h - 16 * q) % LANES
                moved = pltpu.roll(picked, shift, 1) if shift else picked
                parts_of[q] = jnp.where((lane16 >> 4) == h, moved, parts_of[q])
        flat = jnp.concatenate(parts_of, axis=0)
        lane = lax.broadcasted_iota(jnp.int32, (parts, LANES), 1)
        out_ref[pl.ds(per - 1, parts, stride=per), :] = jnp.where(
            lane < 64, pltpu.roll(flat, 1, 0), pltpu.roll(flat, parts - 1, 0)
        )

    vmem = pl.BlockSpec(memory_space=pltpu.VMEM)
    hbm = pl.BlockSpec(memory_space=pltpu.HBM)
    return pl.pallas_call(
        body,
        name="pack",
        out_shape=jax.ShapeDtypeStruct((parts * per, LANES), jnp.float32),
        in_specs=[hbm, hbm, hbm, hbm],
        out_specs=vmem,
        scratch_shapes=[
            pltpu.SMEM((1, 1), jnp.int32),
            pltpu.SMEM((1, 1), jnp.int32),
            pltpu.VMEM(state.shape, jnp.float32),
            pltpu.VMEM(inputs.shape, jnp.float32),
            pltpu.VMEM((LANES, LANES), jnp.float32),
            pltpu.SemaphoreType.DMA((2 + 2 * pieces,)),
        ],
        compiler_params=pltpu.CompilerParams(vmem_limit_bytes=32 << 20),
    )(block_start, period, *[pltpu.with_memory_space_constraint(v, pltpu.HBM) for v in (state, inputs)])


def iterate(block_start, period, received, dynamics, gain, inverse, parts):
    states = dynamics.shape[0]
    controls = gain.shape[1]
    both = states + controls
    width = 2 * LANES
    rows = width + 2 * HALO
    span = states
    run = width // 8
    per = received.shape[0] // parts
    nt = (((1,), (1,)), ((), ()))
    nn = (((1,), (0,)), ((), ()))
    tn = (((0,), (0,)), ((), ()))

    def body(bs_hbm, pe_hbm, got_ref, a_ref, b_ref, k_ref, x_ref, u_ref, z_ref, sums_ref,
             bs_ref, pe_ref, sems, nd_ref, ys_ref, vs_ref, gn_ref, ab_ref, *tiled):
        scalars = [
            pltpu.make_async_copy(bs_hbm, bs_ref, sems.at[0]),
            pltpu.make_async_copy(pe_hbm, pe_ref, sems.at[1]),
        ]
        for copy in scalars:
            copy.start()
        tiles = states // LANES
        neg_refs = tiled[: both // LANES]
        ws_refs = tiled[both // LANES : 2 * both // LANES]
        zs_refs = tiled[2 * both // LANES :]
        sub = lax.broadcasted_iota(jnp.int32, (8, LANES), 0)
        edge_row = lax.broadcasted_iota(jnp.int32, (8, states), 0)

        def lay(half, at, columns):
            for i in range(LANES // run):
                to = pl.ds(half * (LANES // run) + i, run, stride=8)
                neg_refs[at // LANES][to, :] = columns[run * i : run * i + run]

        def in_order(ref):
            return jnp.concatenate([ref[pl.ds(i, run, stride=8), :] for i in range(8)], axis=0)

        def keep_in(refs, values):
            for k, ref in enumerate(refs):
                ref[...] = values[:width, LANES * k : LANES * k + LANES]

        def joined(refs):
            return jnp.concatenate([ref[...] for ref in refs], axis=1)

        def back(values):
            near = pltpu.roll(values[width - 8 : width], 1, 0)
            halo = pltpu.roll(values[width:], 1, 0)
            begin = jnp.where(edge_row == 0, halo, near)
            return jnp.concatenate([begin, values[: width - 8], jnp.where(edge_row == 0, near, halo)], axis=0)

        def onward(values):
            near = pltpu.roll(values[:8], 7, 0)
            halo = pltpu.roll(values[width:], 7, 0)
            end = jnp.where(edge_row == 7, halo, near)
            return jnp.concatenate([values[8:width], end, jnp.where(edge_row == 7, near, halo)], axis=0)

        for g in range(states // LANES):
            for j in range(2):
                block = jnp.concatenate(
                    [got_ref[per * s + 8 * j : per * s + 8 * j + 8, :] for s in range(16 * g, 16 * g + 16)], axis=0
                )
                lay(j, LANES * g, -block.T)
        for g in range(controls // LANES):
            halves = ([], [])
            for s in range(32 * g, 32 * g + 32, 2):
                one = got_ref[per * s + 16 : per * s + 24, :]
                two = got_ref[per * (s + 1) + 16 : per * (s + 1) + 24, :]
                halves[0].append(jnp.where(sub < 4, one, pltpu.roll(two, 4, 0)))
                halves[1].append(jnp.where(sub < 4, pltpu.roll(one, 4, 0), two))
            for j in range(2):
                at = states + LANES * g
                lay(j, at, -jnp.concatenate(halves[j], axis=0).T)
        edge = got_ref[pl.ds(per - 1, parts, stride=per), :]
        high = edge.astype(jnp.bfloat16)
        rest = edge - high.astype(jnp.float32)
        middle = rest.astype(jnp.bfloat16)
        low = (rest - middle.astype(jnp.float32)).astype(jnp.bfloat16)
        cut = jnp.concatenate([high, middle, low], axis=0)
        src = lax.broadcasted_iota(jnp.int32, (3 * parts, both), 0) & (parts - 1)
        col = lax.broadcasted_iota(jnp.int32, (3 * parts, both), 1)
        owner = jnp.where(col < states, col >> 3, (col - states) >> 2)
        spread = jnp.where(owner == src, 1.0, 0.0).astype(jnp.bfloat16)
        wide = lax.dot_general(cut, spread, tn, preferred_element_type=jnp.float32)
        slot = lax.broadcasted_iota(jnp.int32, (LANES, both), 0) & 15
        col = lax.broadcasted_iota(jnp.int32, (LANES, both), 1)
        place = jnp.where(col < states, col & 7, 8 + (col & 3))
        wide = jnp.where(slot == place, wide, 0.0).reshape(8, 16, both).sum(axis=1)
        wide = -pltpu.roll(wide, HALO, 0)
        for k, ref in enumerate(neg_refs):
            ref[width : width + 8, :] = wide[:, LANES * k : LANES * k + LANES]

        ab_ref[:, :states] = a_ref[...]
        ab_ref[:, states:] = b_ref[...]
        for it in range(ITERS):
            last = it == ITERS - 1
            if it == 0:
                rhs = joined(neg_refs).astype(jnp.bfloat16)
            else:
                g = gn_ref[...]
                t = lax.dot_general(g, ab_ref[...], nn, preferred_element_type=jnp.float32)
                rhs = jnp.concatenate(
                    [
                        (nd_ref[...] + RHO * t[:, :states]).astype(jnp.bfloat16),
                        (joined(neg_refs[tiles:]) + RHO * t[:, states:]).astype(jnp.bfloat16),
                    ],
                    axis=1,
                )
            w = lax.dot_general(rhs, k_ref[...], nt, preferred_element_type=jnp.float32)
            wb = w.astype(jnp.bfloat16)
            primal, dual = 0.0, 0.0
            if last:
                for copy in scalars:
                    copy.wait()
                idx = lax.rem(lax.axis_index("section") - bs_ref[0, 0] + parts, parts)
                count = pe_ref[0, 0] - idx * width
                row = lax.broadcasted_iota(jnp.int32, (width, span), 0)
                here = run * (row & 7) + (row >> 3) < count
                keep = lax.broadcasted_iota(jnp.int32, (LANES, width), 1) < count
                keep_in(ws_refs, w)
                for k in range(controls // LANES):
                    u_ref[LANES * k : LANES * k + LANES, :] = jnp.where(keep, in_order(ws_refs[tiles + k]).T, 0.0)
            for n in range(0, states, span):
                at = slice(n, n + span)
                x = w[:, at]
                pred = lax.dot_general(wb, ab_ref[at, :], nt, preferred_element_type=jnp.float32)
                if it == 0:
                    a, p = x, pred
                else:
                    a, p = x + ys_ref[:, at], pred + vs_ref[:, at]
                znew = 0.5 * (a + back(p))
                znn = onward(znew)
                if not last:
                    y = a - znew
                    v = p - znn
                    ys_ref[:, at] = y
                    vs_ref[:, at] = v
                    gn_ref[:, at] = (znn - v).astype(jnp.bfloat16)
                    nd_ref[:, at] = joined(neg_refs[:tiles]) + RHO * (znew - y)
                    if it == ITERS - 2:
                        keep_in(zs_refs, znew)
                else:
                    gap = (x - znew)[:width]
                    miss = (pred - znn)[:width]
                    step = znew[:width] - joined(zs_refs)
                    primal += jnp.sum(jnp.where(here, gap * gap + miss * miss, 0.0), axis=0, keepdims=True)
                    dual += RHO * RHO * jnp.sum(jnp.where(here, step * step, 0.0), axis=0, keepdims=True)
                    keep_in(zs_refs, znew)
                    for k in range(tiles):
                        to = slice(LANES * k, LANES * k + LANES)
                        x_ref[to, :] = jnp.where(keep, in_order(ws_refs[k]).T, 0.0)
                        z_ref[to, :] = jnp.where(keep, in_order(zs_refs[k]).T, 0.0)
            if last:
                lane = lax.broadcasted_iota(jnp.int32, (parts, LANES), 1)
                sums_ref[...] = jnp.where(lane == 0, jnp.sum(primal), jnp.where(lane == 1, jnp.sum(dual), 0.0))

    hbm = pl.BlockSpec(memory_space=pltpu.HBM)
    vmem = pl.BlockSpec(memory_space=pltpu.VMEM)
    return pl.pallas_call(
        body,
        name="iterate",
        out_shape=(
            pltpu.VMEM((states, width), jnp.float32),
            pltpu.VMEM((controls, width), jnp.float32),
            pltpu.VMEM((states, width), jnp.float32),
            jax.ShapeDtypeStruct((parts, LANES), jnp.float32),
        ),
        in_specs=[hbm, hbm, vmem, vmem, vmem, vmem],
        out_specs=(vmem, vmem, vmem, vmem),
        scratch_shapes=[
            pltpu.SMEM((1, 1), jnp.int32),
            pltpu.SMEM((1, 1), jnp.int32),
            pltpu.SemaphoreType.DMA((2,)),
            pltpu.VMEM((rows, states), jnp.float32),
            pltpu.VMEM((rows, states), jnp.float32),
            pltpu.VMEM((rows, states), jnp.float32),
            pltpu.VMEM((rows, states), jnp.bfloat16),
            pltpu.VMEM((states, both), jnp.bfloat16),
            *[pltpu.VMEM((rows, LANES), jnp.float32)] * (both // LANES),
            *[pltpu.VMEM((width, LANES), jnp.float32)] * ((both + states) // LANES),
        ],
        compiler_params=pltpu.CompilerParams(vmem_limit_bytes=48 << 20),
    )(
        block_start,
        period,
        received,
        dynamics,
        gain,
        inverse,
    )


def finish(sums, *blocks):
    def body(sums_ref, *refs):
        sources, sinks = refs[: len(blocks)], refs[len(blocks) : 2 * len(blocks)]
        norms_hbm, norms_ref, sems = refs[-3:]
        copies = [pltpu.make_async_copy(a, b, sems.at[i]) for i, (a, b) in enumerate(zip(sources, sinks))]
        for copy in copies:
            copy.start()
        norms_ref[...] = jnp.sqrt(jnp.sum(sums_ref[...], axis=0, keepdims=True))[:, :2]
        copies.append(pltpu.make_async_copy(norms_ref, norms_hbm, sems.at[len(blocks)]))
        copies[-1].start()
        for copy in copies:
            copy.wait()

    vmem = pl.BlockSpec(memory_space=pltpu.VMEM)
    hbm = pl.BlockSpec(memory_space=pltpu.HBM)
    return pl.pallas_call(
        body,
        name="finish",
        out_shape=(
            *[pltpu.HBM(b.shape, b.dtype) for b in blocks],
            pltpu.HBM((1, 2), jnp.float32),
        ),
        in_specs=[vmem] * (1 + len(blocks)),
        out_specs=(*[hbm] * len(blocks), hbm),
        scratch_shapes=[pltpu.VMEM((1, 2), jnp.float32), pltpu.SemaphoreType.DMA((len(blocks) + 1,))],
    )(*[pltpu.with_memory_space_constraint(b, pltpu.VMEM) for b in (sums, *blocks)])


def swap(rows, parts):
    flat = rows.reshape(parts, 1, rows.size // parts)
    return lax.all_to_all(flat, "section", 0, 0, tiled=True)


def local(dynamics, gain, inverse, lin_state, lin_input, block_start, period):
    parts = lax.axis_size("section")
    block_start, period = block_start[None], period[None]
    packed = pack(block_start, period, lin_state, lin_input, parts)
    received = swap(packed, parts).reshape(packed.shape)
    x, u, z, sums = iterate(block_start, period, received, dynamics, gain, inverse, parts)
    sums = swap(sums, parts).reshape(sums.shape)
    x, u, z, norms = finish(sums, x, u, z)
    return x, u, z, norms.reshape(2)


def solution(mesh):
    return jax.shard_map(
        local,
        mesh=mesh,
        in_specs=(
            P("plant", None),
            P("plant", None),
            P("plant", None),
            P(("plant", "section"), None),
            P(("plant", "section"), None),
            P("plant"),
            P("plant"),
        ),
        out_specs=(P("plant", "section"), P("plant", "section"), P("plant", "section"), P("plant")),
        check_vma=False,
    )
```

```python
import jax
import jax.numpy as jnp
from jax import lax
from jax.experimental import pallas as pl
from jax.experimental.pallas import tpu as pltpu
from jax.sharding import PartitionSpec as P

ITERS = 4
RHO = 1.0
LANES = 128
HALO = 4


def pack(block_start, period, state, inputs, parts):
    rows_state, total = state.shape
    rows_input = inputs.shape[0]
    width = total // parts
    per = 2 * rows_state + 2 * rows_input + 1
    assert width == 2 * LANES and rows_state == 8 and rows_input == 4

    pieces = 2
    piece = total // pieces

    def body(bs_ref, pe_ref, st_hbm, in_hbm, out_ref, st_ref, in_ref, st_first, in_first, sems):
        bs = bs_ref[0]
        pe = pe_ref[0]
        opening = pl.ds(pl.multiple_of(bs * width, LANES), LANES)
        copies = [
            pltpu.make_async_copy(st_hbm.at[:, opening], st_first, sems.at[0]),
            pltpu.make_async_copy(in_hbm.at[:, opening], in_first, sems.at[1]),
        ]
        for q in range(pieces):
            at = slice(piece * q, piece * q + piece)
            copies.append(pltpu.make_async_copy(st_hbm.at[:, at], st_ref.at[:, at], sems.at[2 + 2 * q]))
            copies.append(pltpu.make_async_copy(in_hbm.at[:, at], in_ref.at[:, at], sems.at[3 + 2 * q]))
        for copy in copies:
            copy.start()
        lane = lax.broadcasted_iota(jnp.int32, (16, LANES), 1)
        spare = jnp.zeros((4, LANES), jnp.float32)

        def tile(position):
            at = pl.ds(pl.multiple_of(position, LANES), LANES)
            return jnp.concatenate([st_ref[:, at], in_ref[:, at], spare], axis=0)

        copies[0].wait()
        copies[1].wait()
        first = jnp.concatenate([st_first[...], in_first[...], spare], axis=0)
        onward = pltpu.roll(first, lax.rem(pe, LANES), 1)
        edges = []
        for q in range(4):
            if q * pieces % 4 == 0:
                copies[2 + 2 * (q * pieces // 4)].wait()
                copies[3 + 2 * (q * pieces // 4)].wait()
            collected = jnp.zeros((16, LANES), jnp.float32)
            for e in range(16):
                d = 16 * q + e
                ends = []
                for half in range(2):
                    at = (2 * d + half) * LANES
                    section = lax.rem(at - bs * width + total, total)
                    beyond = lane + (section - pe)
                    wraps = (beyond >= 0) & (beyond < HALO)
                    cut = jnp.where(wraps, onward, tile(at))
                    out_ref[per * d + 8 * half : per * d + 8 * half + 8, :] = cut[:8]
                    out_ref[per * d + 16 + 4 * half : per * d + 20 + 4 * half, :] = cut[8:12]
                    ends.append(cut)
                both = jnp.where(lane < HALO, ends[0], ends[1])
                shift = (8 * e + HALO) % LANES
                both = pltpu.roll(both, shift, 1) if shift else both
                collected = jnp.where((lane >> 3) == e, both, collected)
            edges.append(collected)
        before = lax.rem(bs + parts - 1, parts)
        late = lax.rem(pe - HALO, LANES)
        tail_at = lax.rem(pe - HALO - late + bs * width, total)
        tail_next = lax.rem(tail_at + LANES, total)
        tail = jnp.where(lane >= late, tile(tail_at), tile(tail_next))
        tail = pltpu.roll(tail, lax.rem(8 * lax.rem(before, 16) - late + LANES, LANES), 1)
        skip = total - pe
        skip = jnp.where(skip < HALO, skip, 0)
        head = pltpu.roll(first, lax.rem(8 * lax.rem(bs, 16) + HALO - skip + LANES, LANES), 1)
        values = []
        for q in range(4):
            block = 16 * q + (lane >> 3)
            slot = lane & 7
            value = jnp.where((block == before) & (slot < HALO), tail, edges[q])
            values.append(jnp.where((block == bs) & (slot >= HALO), head, value))
        slots = [jnp.where((lane & 7) == h, 1.0, 0.0).astype(jnp.bfloat16) for h in range(8)]
        device = lax.broadcasted_iota(jnp.int32, (16, LANES), 0)
        pick = jnp.where((lane >> 3) == device, 1.0, 0.0).astype(jnp.bfloat16)
        pick = jnp.concatenate([pick, pick, pick], axis=1)
        parts_of = []
        for value in values:
            high = value.astype(jnp.bfloat16)
            rest = value - high.astype(jnp.float32)
            middle = rest.astype(jnp.bfloat16)
            low = (rest - middle.astype(jnp.float32)).astype(jnp.bfloat16)
            spread = [jnp.concatenate([part * slot for slot in slots], axis=0) for part in (high, middle, low)]
            parts_of.append(
                lax.dot_general(
                    pick,
                    jnp.concatenate(spread, axis=1),
                    (((1,), (1,)), ((), ())),
                    preferred_element_type=jnp.float32,
                )
            )
        flat = jnp.concatenate(parts_of, axis=0)
        lane = lax.broadcasted_iota(jnp.int32, (parts, LANES), 1)
        out_ref[pl.ds(per - 1, parts, stride=per), :] = jnp.where(
            lane < 64, pltpu.roll(flat, 1, 0), pltpu.roll(flat, parts - 1, 0)
        )

    smem = pl.BlockSpec(memory_space=pltpu.SMEM)
    vmem = pl.BlockSpec(memory_space=pltpu.VMEM)
    hbm = pl.BlockSpec(memory_space=pltpu.HBM)
    return pl.pallas_call(
        body,
        name="pack",
        out_shape=jax.ShapeDtypeStruct((parts * per, LANES), jnp.float32),
        in_specs=[smem, smem, hbm, hbm],
        out_specs=vmem,
        scratch_shapes=[
            pltpu.VMEM(state.shape, jnp.float32),
            pltpu.VMEM(inputs.shape, jnp.float32),
            pltpu.VMEM((rows_state, LANES), jnp.float32),
            pltpu.VMEM((rows_input, LANES), jnp.float32),
            pltpu.SemaphoreType.DMA((2 + 2 * pieces,)),
        ],
        compiler_params=pltpu.CompilerParams(vmem_limit_bytes=32 << 20),
    )(
        block_start,
        period,
        pltpu.with_memory_space_constraint(state, pltpu.HBM),
        pltpu.with_memory_space_constraint(inputs, pltpu.HBM),
    )


def iterate(block_start, period, received, dynamics, gain, inverse, parts):
    states = dynamics.shape[0]
    controls = gain.shape[1]
    both = states + controls
    width = 2 * LANES
    rows = width + 2 * HALO
    span = states
    run = width // 8
    per = received.shape[0] // parts
    nt = (((1,), (1,)), ((), ()))
    nn = (((1,), (0,)), ((), ()))
    tn = (((0,), (0,)), ((), ()))

    def body(bs_ref, pe_ref, got_ref, a_ref, b_ref, k_ref, x_ref, u_ref, z_ref, sums_ref,
             nd_ref, ys_ref, vs_ref, gn_ref, ab_ref, *tiled):
        tiles = states // LANES
        neg_refs = tiled[: both // LANES]
        ws_refs = tiled[both // LANES : 2 * both // LANES]
        zs_refs = tiled[2 * both // LANES :]
        sub = lax.broadcasted_iota(jnp.int32, (8, LANES), 0)
        edge_row = lax.broadcasted_iota(jnp.int32, (8, states), 0)

        def lay(half, at, columns):
            for i in range(LANES // run):
                to = pl.ds(half * (LANES // run) + i, run, stride=8)
                neg_refs[at // LANES][to, :] = columns[run * i : run * i + run]

        def in_order(ref):
            return jnp.concatenate([ref[pl.ds(i, run, stride=8), :] for i in range(8)], axis=0)

        def keep_in(refs, values):
            for k, ref in enumerate(refs):
                ref[...] = values[:width, LANES * k : LANES * k + LANES]

        def joined(refs):
            return jnp.concatenate([ref[...] for ref in refs], axis=1)

        def back(values):
            near = pltpu.roll(values[width - 8 : width], 1, 0)
            halo = pltpu.roll(values[width:], 1, 0)
            begin = jnp.where(edge_row == 0, halo, near)
            return jnp.concatenate([begin, values[: width - 8], jnp.where(edge_row == 0, near, halo)], axis=0)

        def onward(values):
            near = pltpu.roll(values[:8], 7, 0)
            halo = pltpu.roll(values[width:], 7, 0)
            end = jnp.where(edge_row == 7, halo, near)
            return jnp.concatenate([values[8:width], end, jnp.where(edge_row == 7, near, halo)], axis=0)

        for g in range(states // LANES):
            for j in range(2):
                block = jnp.concatenate(
                    [got_ref[per * s + 8 * j : per * s + 8 * j + 8, :] for s in range(16 * g, 16 * g + 16)], axis=0
                )
                lay(j, LANES * g, -block.T)
        for g in range(controls // LANES):
            halves = ([], [])
            for s in range(32 * g, 32 * g + 32, 2):
                one = got_ref[per * s + 16 : per * s + 24, :]
                two = got_ref[per * (s + 1) + 16 : per * (s + 1) + 24, :]
                halves[0].append(jnp.where(sub < 4, one, pltpu.roll(two, 4, 0)))
                halves[1].append(jnp.where(sub < 4, pltpu.roll(one, 4, 0), two))
            for j in range(2):
                at = states + LANES * g
                lay(j, at, -jnp.concatenate(halves[j], axis=0).T)
        edge = got_ref[pl.ds(per - 1, parts, stride=per), :]
        high = edge.astype(jnp.bfloat16)
        rest = edge - high.astype(jnp.float32)
        middle = rest.astype(jnp.bfloat16)
        low = (rest - middle.astype(jnp.float32)).astype(jnp.bfloat16)
        cut = jnp.concatenate([high, middle, low], axis=0)
        src = lax.broadcasted_iota(jnp.int32, (3 * parts, both), 0) & (parts - 1)
        col = lax.broadcasted_iota(jnp.int32, (3 * parts, both), 1)
        owner = jnp.where(col < states, col >> 3, (col - states) >> 2)
        spread = jnp.where(owner == src, 1.0, 0.0).astype(jnp.bfloat16)
        wide = lax.dot_general(cut, spread, tn, preferred_element_type=jnp.float32)
        slot = lax.broadcasted_iota(jnp.int32, (LANES, both), 0) & 15
        col = lax.broadcasted_iota(jnp.int32, (LANES, both), 1)
        place = jnp.where(col < states, col & 7, 8 + (col & 3))
        wide = jnp.where(slot == place, wide, 0.0).reshape(8, 16, both).sum(axis=1)
        wide = -pltpu.roll(wide, HALO, 0)
        for k, ref in enumerate(neg_refs):
            ref[width : width + 8, :] = wide[:, LANES * k : LANES * k + LANES]

        ab_ref[:, :states] = a_ref[...]
        ab_ref[:, states:] = b_ref[...]
        for it in range(ITERS):
            last = it == ITERS - 1
            if it == 0:
                rhs = joined(neg_refs).astype(jnp.bfloat16)
            else:
                g = gn_ref[...]
                t = lax.dot_general(g, ab_ref[...], nn, preferred_element_type=jnp.float32)
                rhs = jnp.concatenate(
                    [
                        (nd_ref[...] + RHO * t[:, :states]).astype(jnp.bfloat16),
                        (joined(neg_refs[tiles:]) + RHO * t[:, states:]).astype(jnp.bfloat16),
                    ],
                    axis=1,
                )
            w = lax.dot_general(rhs, k_ref[...], nt, preferred_element_type=jnp.float32)
            wb = w.astype(jnp.bfloat16)
            primal, dual = 0.0, 0.0
            if last:
                idx = lax.rem(lax.axis_index("section") - bs_ref[0] + parts, parts)
                count = pe_ref[0] - idx * width
                row = lax.broadcasted_iota(jnp.int32, (width, span), 0)
                here = run * (row & 7) + (row >> 3) < count
                keep = lax.broadcasted_iota(jnp.int32, (LANES, width), 1) < count
                keep_in(ws_refs, w)
                for k in range(controls // LANES):
                    u_ref[LANES * k : LANES * k + LANES, :] = jnp.where(keep, in_order(ws_refs[tiles + k]).T, 0.0)
            for n in range(0, states, span):
                at = slice(n, n + span)
                x = w[:, at]
                pred = lax.dot_general(wb, ab_ref[at, :], nt, preferred_element_type=jnp.float32)
                if it == 0:
                    a, p = x, pred
                else:
                    a, p = x + ys_ref[:, at], pred + vs_ref[:, at]
                znew = 0.5 * (a + back(p))
                znn = onward(znew)
                if not last:
                    y = a - znew
                    v = p - znn
                    ys_ref[:, at] = y
                    vs_ref[:, at] = v
                    gn_ref[:, at] = (znn - v).astype(jnp.bfloat16)
                    nd_ref[:, at] = joined(neg_refs[:tiles]) + RHO * (znew - y)
                    if it == ITERS - 2:
                        keep_in(zs_refs, znew)
                else:
                    gap = (x - znew)[:width]
                    miss = (pred - znn)[:width]
                    step = znew[:width] - joined(zs_refs)
                    primal += jnp.sum(jnp.where(here, gap * gap + miss * miss, 0.0), axis=0, keepdims=True)
                    dual += RHO * RHO * jnp.sum(jnp.where(here, step * step, 0.0), axis=0, keepdims=True)
                    keep_in(zs_refs, znew)
                    for k in range(tiles):
                        to = slice(LANES * k, LANES * k + LANES)
                        x_ref[to, :] = jnp.where(keep, in_order(ws_refs[k]).T, 0.0)
                        z_ref[to, :] = jnp.where(keep, in_order(zs_refs[k]).T, 0.0)
            if last:
                lane = lax.broadcasted_iota(jnp.int32, (parts, LANES), 1)
                sums_ref[...] = jnp.where(lane == 0, jnp.sum(primal), jnp.where(lane == 1, jnp.sum(dual), 0.0))

    smem = pl.BlockSpec(memory_space=pltpu.SMEM)
    vmem = pl.BlockSpec(memory_space=pltpu.VMEM)
    return pl.pallas_call(
        body,
        name="iterate",
        out_shape=(
            pltpu.VMEM((states, width), jnp.float32),
            pltpu.VMEM((controls, width), jnp.float32),
            pltpu.VMEM((states, width), jnp.float32),
            jax.ShapeDtypeStruct((parts, LANES), jnp.float32),
        ),
        in_specs=[smem, smem, vmem, vmem, vmem, vmem],
        out_specs=(vmem, vmem, vmem, vmem),
        scratch_shapes=[
            pltpu.VMEM((rows, states), jnp.float32),
            pltpu.VMEM((rows, states), jnp.float32),
            pltpu.VMEM((rows, states), jnp.float32),
            pltpu.VMEM((rows, states), jnp.bfloat16),
            pltpu.VMEM((states, both), jnp.bfloat16),
            *[pltpu.VMEM((rows, LANES), jnp.float32)] * (both // LANES),
            *[pltpu.VMEM((width, LANES), jnp.float32)] * ((both + states) // LANES),
        ],
        compiler_params=pltpu.CompilerParams(vmem_limit_bytes=48 << 20),
    )(block_start, period, received, dynamics, gain, inverse)


def finish(sums, *blocks):
    def body(sums_ref, *refs):
        sources, sinks = refs[: len(blocks)], refs[len(blocks) : 2 * len(blocks)]
        norms_hbm, norms_ref, sems = refs[-3:]
        copies = [pltpu.make_async_copy(a, b, sems.at[i]) for i, (a, b) in enumerate(zip(sources, sinks))]
        for copy in copies:
            copy.start()
        norms_ref[...] = jnp.sqrt(jnp.sum(sums_ref[...], axis=0, keepdims=True))[:, :2]
        copies.append(pltpu.make_async_copy(norms_ref, norms_hbm, sems.at[len(blocks)]))
        copies[-1].start()
        for copy in copies:
            copy.wait()

    vmem = pl.BlockSpec(memory_space=pltpu.VMEM)
    hbm = pl.BlockSpec(memory_space=pltpu.HBM)
    return pl.pallas_call(
        body,
        name="finish",
        out_shape=(
            *[pltpu.HBM(b.shape, b.dtype) for b in blocks],
            pltpu.HBM((1, 2), jnp.float32),
        ),
        in_specs=[vmem] * (1 + len(blocks)),
        out_specs=(*[hbm] * len(blocks), hbm),
        scratch_shapes=[pltpu.VMEM((1, 2), jnp.float32), pltpu.SemaphoreType.DMA((len(blocks) + 1,))],
    )(*[pltpu.with_memory_space_constraint(b, pltpu.VMEM) for b in (sums, *blocks)])


def swap(rows, parts):
    flat = rows.reshape(parts, 1, rows.size // parts)
    return lax.all_to_all(flat, "section", 0, 0, tiled=True)


def local(dynamics, gain, inverse, lin_state, lin_input, block_start, period):
    parts = lax.axis_size("section")
    packed = pack(block_start, period, lin_state, lin_input, parts)
    received = swap(packed, parts).reshape(packed.shape)
    x, u, z, sums = iterate(block_start, period, received, dynamics, gain, inverse, parts)
    sums = swap(sums, parts).reshape(sums.shape)
    x, u, z, norms = finish(sums, x, u, z)
    return x, u, z, norms.reshape(2)


def solution(mesh):
    return jax.shard_map(
        local,
        mesh=mesh,
        in_specs=(
            P("plant", None),
            P("plant", None),
            P("plant", None),
            P(("plant", "section"), None),
            P(("plant", "section"), None),
            P("plant"),
            P("plant"),
        ),
        out_specs=(P("plant", "section"), P("plant", "section"), P("plant", "section"), P("plant")),
        check_vma=False,
    )
```
